512 devices in a mesh: seq: 64 (over x, z, core), head: 8 (over y).
Axes of the slice: x: 4, y: 8, z: 8, core: 2. Of those that a mesh axis runs over, the one named last changes fastest.
Arguments:
- queries: bfloat16 [16384, 4096], P('seq', 'head'), may hold values from -6 to 6
- keys: bfloat16 [16384, 4096], P('seq', 'head'), may hold values from -6 to 6
- values: bfloat16 [16384, 4096], P('seq', 'head'), may hold values from -6 to 6
- gate: bfloat16 [16384, 4096], P('seq', 'head'), may hold values from -6 to 6
- residual: bfloat16 [16384, 4096], P('seq', 'head'), may hold values from -40 to 40
- log_decay: float32 [16384, 32], P('seq', 'head'), may hold values from -1 to 0, as said below
- out_weight: bfloat16 [4096, 4096], P('seq', 'head'), may hold values from -0.09375 to 0.09375
- norm_gain: bfloat16 [4096], P('head'), may hold values from 0.099609375 to 1.8984375
- kv_weight: bfloat16 [4096, 2048], P('seq', 'head'), may hold values from -0.09375 to 0.09375
Outputs:
- cache_keys: bfloat16 [16384, 1024], P('seq', 'head')
- cache_values: bfloat16 [16384, 1024], P('seq', 'head')
The draws below stay inside these ranges and needn't reach their ends.
Inputs may be any that keep to these rules, and one draw needn't show every extreme that they name: `log_decay`: every entry is negative.
All inputs are finite; a program needn't handle non-finite values.
Results may differ from the reference program's by a relative error of at most 0.015.
Values may be sent and summed in bfloat16 or wider, within the bound.
A program may use at most 64 MiB of HBM per device.

```python
import math
import jax
import jax.numpy as jnp
from jax import lax

H = 32
HD = 128
KV_HEADS = 8
D = 4096
TOK_DEV = 256
LEADING_WORDS = 16384


def draw_log_decay(key, part):
    parts_list = jax.random.split(key, 6)
    share = 0.5
    fast = jax.random.uniform(parts_list[0], (H,)) < share
    fast_rate = 1.0 / 40.0 * jnp.exp(jax.random.uniform(parts_list[1], (H,), minval=-0.35, maxval=0.35))
    slow_rate = 0.5 / LEADING_WORDS * jnp.exp(jax.random.uniform(parts_list[1], (H,), minval=-0.5, maxval=0.4))
    fading_ratio = jnp.where(fast, fast_rate, slow_rate)
    segment_scaling = jnp.exp(jax.random.uniform(parts_list[2], (LEADING_WORDS // TOK_DEV, H), minval=-0.7, maxval=0.7))
    segment_scaling = jnp.repeat(segment_scaling, TOK_DEV, axis=0)
    item_scaling = jnp.exp(jax.random.uniform(parts_list[3], (LEADING_WORDS, H), minval=-0.5, maxval=0.5))
    index_places = jax.random.randint(parts_list[4], (2,), 0, LEADING_WORDS)
    copy_packet = jnp.any(jnp.arange(LEADING_WORDS)[:, None] == index_places[None, :], axis=1).astype(jnp.float32)
    entry_tally = jax.random.uniform(parts_list[5], (LEADING_WORDS, H), minval=0.22, maxval=0.6)
    layer_answer = -(fading_ratio[None, :] * segment_scaling * item_scaling) - copy_packet[:, None] * entry_tally
    return layer_answer.astype(jnp.float32)


def draw_residual(key, part):
    parts_list = jax.random.split(key, 2)
    column = jnp.arange(D, dtype=jnp.float32) / (D - 1)
    colscale = 0.4 * jnp.exp(column * math.log(5.0)) * jax.random.uniform(parts_list[1], (D,), minval=0.7, maxval=1.3)
    base = jnp.clip(jax.random.normal(parts_list[0], (LEADING_WORDS, D)), -6.0, 6.0)
    layer_answer = base * colscale[None, :]
    return layer_answer.astype(jnp.bfloat16)


def steps_of(stream_key, dims, pieces, low, top_value):
    def one(dim, shards_of):
        steps = jax.random.uniform(jax.random.fold_in(jax.random.fold_in(stream_key, 6), dim), (shards_of,), jnp.float32, low / len(pieces), top_value / len(pieces))
        return jnp.repeat(jnp.exp(steps), dims[dim] // shards_of).reshape((-1,) + (1,) * (len(dims) - dim - 1))

    factor_of = one(*pieces[0])
    for cut in pieces[1:]:
        factor_of = factor_of * one(*cut)
    return factor_of


def gaussian(rng, dims, scale, limit, cuts=(), kind=jnp.bfloat16):
    level = steps_of(rng, dims, cuts, -0.22, 0.18) if cuts else 1.0
    values = jax.random.normal(rng, dims, jnp.float32) * scale * level
    return jnp.minimum(jnp.maximum(values, -limit), limit).astype(kind)


def setup_inputs(seed: int = 0) -> dict:
    key_list = jax.random.split(jax.random.key(seed), 10)
    return {
        "queries": gaussian(key_list[0], (LEADING_WORDS, D), 1.0, 6.0, ((0, 64), (1, 8))),
        "keys": gaussian(key_list[1], (LEADING_WORDS, D), 1.0, 6.0, ((0, 64), (1, 8))),
        "values": gaussian(key_list[2], (LEADING_WORDS, D), 1.0, 6.0, ((0, 64), (1, 8))),
        "gate": gaussian(key_list[3], (LEADING_WORDS, D), 1.0, 6.0, ((0, 64), (1, 8))),
        "residual": draw_residual(jax.random.fold_in(key_list[9], 71), 0),
        "log_decay": draw_log_decay(jax.random.fold_in(key_list[9], 71), 0),
        "out_weight": gaussian(key_list[6], (D, D), D ** -0.5, 0.09375, ((0, 64), (1, 8))),
        "norm_gain": jnp.clip(1.0 + 0.18 * jax.random.normal(key_list[7], (D,), jnp.float32), 0.099609375, 1.8984375).astype(jnp.bfloat16),
        "kv_weight": gaussian(key_list[8], (D, 2 * KV_HEADS * HD), D ** -0.5, 0.09375, ((0, 64), (1, 8))),
    }


HIGHEST = lax.Precision.HIGHEST

def local_retention(queries, keys, values, log_decay, block):
    tokens, heads, width = queries.shape
    count = tokens // block

    def to_blocks(array):
        return array.reshape((count, block) + array.shape[1:])
    lower = jnp.arange(block)[:, None] >= jnp.arange(block)[None, :]

    def advance(carry, inputs):
        state, offset = carry
        query_block, key_block, value_block, decay_block = inputs
        within = jnp.cumsum(decay_block, axis=0)
        spread = within[:, None, :] - within[None, :, :]
        factor = jnp.where(lower[:, :, None], jnp.exp(jnp.where(lower[:, :, None], spread, 0.0)), 0.0)
        scores = jnp.einsum('ihd,jhd->hij', query_block.astype(jnp.float32), key_block.astype(jnp.float32), precision=HIGHEST)
        weighted = scores * jnp.transpose(factor, (2, 0, 1))
        values_wide = value_block.astype(jnp.float32)
        intra = jnp.einsum('hij,jhd->ihd', weighted, values_wide, precision=HIGHEST)
        query_wide = query_block.astype(jnp.float32)
        carried = jnp.exp(within)[:, :, None] * jnp.einsum('ihd,hde->ihe', query_wide, state, precision=HIGHEST)
        ending = within[-1]
        key_wide = key_block.astype(jnp.float32) * jnp.exp(ending[None, :] - within)[:, :, None]
        fresh = jnp.exp(ending)[:, None, None] * state + jnp.einsum('jhd,jhe->hde', key_wide, values_wide, precision=HIGHEST)
        return ((fresh, offset + ending), (intra + carried, offset[None, :] + within))
    start = (jnp.zeros((heads, width, width), jnp.float32), jnp.zeros((heads,), jnp.float32))
    final, stacked = lax.scan(advance, start, (to_blocks(queries), to_blocks(keys), to_blocks(values), to_blocks(log_decay)))
    return (stacked[0].reshape(tokens, heads, width), stacked[1].reshape(tokens, heads), final[0], final[1])

def reference(queries, keys, values, gate, residual, log_decay, out_weight, norm_gain, kv_weight):
    shaped = [array.reshape(LEADING_WORDS, H, HD) for array in (queries, keys, values)]
    retained, running, state, offset = local_retention(shaped[0], shaped[1], shaped[2], log_decay, min(512, LEADING_WORDS))
    scale = lax.rsqrt(lax.optimization_barrier(jnp.mean(retained * retained, axis=2, keepdims=True)) + 1e-06)
    mixed = (jax.nn.silu(gate.astype(jnp.float32)) * (retained * scale).reshape(LEADING_WORDS, D)).astype(jnp.bfloat16)
    branch = jnp.dot(mixed, out_weight, preferred_element_type=jnp.float32)
    hidden = (residual.astype(jnp.float32) + branch).astype(jnp.bfloat16)
    wide = hidden.astype(jnp.float32)
    inverse = lax.rsqrt(lax.optimization_barrier(jnp.mean(wide * wide, axis=1, keepdims=True)) + 1e-06)
    normalized = (wide * inverse * norm_gain.astype(jnp.float32)[None, :]).astype(jnp.bfloat16)
    projected = jnp.dot(normalized, kv_weight, preferred_element_type=jnp.float32).reshape(LEADING_WORDS, KV_HEADS, 2, HD)
    cache_keys = projected[:, :, 0, :].reshape(LEADING_WORDS, KV_HEADS * HD).astype(jnp.bfloat16)
    cache_values = projected[:, :, 1, :].reshape(LEADING_WORDS, KV_HEADS * HD).astype(jnp.bfloat16)
    return (cache_keys, cache_values)
```

```python
import functools

import jax
import jax.numpy as jnp
from jax import lax
from jax.experimental import pallas as pl
from jax.experimental.pallas import tpu as pltpu
from jax.sharding import PartitionSpec as P

MESH = pl.DeviceIdType.MESH
HIGHEST = lax.Precision.HIGHEST
F32, BF16 = jnp.float32, jnp.bfloat16

NX, NZ, NC, NY = 4, 8, 2, 8
GROUP = NZ * NC
TOK, WID, HEADS, HD = 256, 512, 4, 128
SLICE = HEADS * HD // GROUP
COPIES = 160
MIX_CHUNKS = 4
MIX_ROWS = TOK // MIX_CHUNKS
RED_CHUNKS = 2
RED_ROWS = TOK // RED_CHUNKS


def dot(a, b, dims=(((1,), (0,)), ((), ())), precision=None):
    return lax.dot_general(a, b, dims, precision=precision, preferred_element_type=F32)


NT = (((1,), (1,)), ((), ()))
TN = (((0,), (0,)), ((), ()))


def layer_kernel(
    q_h, k_h, v_h, g_h, r_h, ld_ref, ow_h, gain_ref, kw_h,
    ok_ref, ov_ref,
    q, k, v, g, res, wbuf, kvb, kin, wcol, st, rs, dec, xs, ex, ob, inc,
    intra, abuf, acc, hg, sr, sl, rr, rl, sq,
    lsem, ssem, rsem,
):
    seq, hy = lax.axis_index("seq"), lax.axis_index("head")
    sx, p = seq // GROUP, lax.rem(seq, GROUP)
    sz, sc = p // NC, lax.rem(p, NC)
    cc = 1 - sc

    def at(x, z, c, y):
        return (lax.rem(x + NX, NX) * GROUP + lax.rem(z + NZ, NZ) * NC + c, lax.rem(y + NY, NY))

    count = [0]
    unsent = []

    def remote(src, dst, device):
        i = count[0]
        count[0] += 1
        copy = pltpu.make_async_remote_copy(
            src_ref=src, dst_ref=dst, send_sem=ssem.at[i], recv_sem=rsem.at[i],
            device_id=device, device_id_type=MESH,
        )
        unsent.append(copy)
        return copy

    def send(src, dst, device):
        copy = remote(src, dst, device)
        copy.start()
        return copy

    def drain(keep=0):
        while len(unsent) > keep:
            unsent.pop(0).wait_send()

    loads = {}
    own_w = wbuf.at[sx, sz, sc]
    for i, (name, src, dst) in enumerate((
        ("k", k_h, k), ("v", v_h, v), ("w", ow_h, own_w), ("kw", kw_h, kin), ("q", q_h, q), ("g", g_h, g), ("r", r_h, res),
    )):
        loads[name] = pltpu.make_async_copy(src, dst, lsem.at[i])
        loads[name].start()

    swap_to = at(lax.rem(sz, NX), hy, cc, 2 * sx + sz // 4)
    swap_from = at(hy // 2, lax.rem(hy, 2) * 4 + sx, cc, sz)
    barrier = pltpu.get_barrier_semaphore()
    group_dev = [(sx * GROUP + lax.rem(p + i, GROUP), hy) for i in range(GROUP)]
    cross_dev = [at(sx + i, sz, sc, hy) for i in range(NX)]
    head_dev = [at(sx, sz, sc, hy + i) for i in range(NY)]
    greeted = group_dev[1:] + cross_dev[1:] + head_dev[1:] + [swap_to, swap_from]
    for device in greeted:
        pl.semaphore_signal(barrier, inc=1, device_id=device, device_id_type=MESH)

    rows = lax.broadcasted_iota(jnp.int32, (TOK, TOK), 0)
    cols = lax.broadcasted_iota(jnp.int32, (TOK, TOK), 1)
    lower = rows >= cols
    ld = jnp.concatenate([ld_ref[...], jnp.zeros((8 - HEADS, TOK), F32)], axis=0)
    wrow = dot(ld, (rows <= cols).astype(F32), precision=HIGHEST)
    within = dot(lower.astype(F32), ld, NT, precision=HIGHEST)
    wcol[...] = within
    dec[p] = jnp.broadcast_to(wrow[:, TOK - 1:TOK], (8, HD))

    pl.semaphore_wait(barrier, len(greeted))

    c_dec = [None] + [send(dec.at[p], dec.at[p], group_dev[i]) for i in range(1, GROUP)]
    loads["w"].wait()
    loads["kw"].wait()
    right_z, left_z = at(sx, sz + 1, sc, hy), at(sx, sz - 1, sc, hy)
    right_x, left_x = at(sx + 1, sz, sc, hy), at(sx - 1, sz, sc, hy)
    right_y, left_y = at(sx, sz, sc, hy + 1), at(sx, sz, sc, hy - 1)
    sibling = at(sx, sz, cc, hy)

    def wz(step, way):
        origin = lax.rem(sz - way * (step - 1) + NZ, NZ)
        if step < NZ // 2:
            part = wbuf.at[sx, origin, sc]
        else:
            part = wbuf.at[sx, origin, sc, pl.ds(0 if way == 1 else 32, 32)]
        return send(part, part, right_z if way == 1 else left_z)

    def wx(step, way):
        origin = lax.rem(sx - way * (step - 1) + NX, NX)
        if step == 1:
            part = wbuf.at[origin, :, sc]
        else:
            part = wbuf.at[origin, pl.ds(0 if way == 1 else NZ // 2, NZ // 2), sc]
        return send(part, part, right_x if way == 1 else left_x)

    def to_sibling(part):
        return send(part, part, sibling)

    def kz(step, way):
        origin = lax.rem(sz - way * (step - 1) + NZ, NZ)
        if step < NZ // 2:
            part = kvb.at[origin, :, cc]
        else:
            part = kvb.at[origin, pl.ds(0 if way == 1 else NX // 2, NX // 2), cc]
        return send(part, part, right_z if way == 1 else left_z)

    c_wz = {(1, way): wz(1, way) for way in (1, -1)}
    c_swap = send(kin, kvb.at[hy, lax.rem(sz, NX), sc], swap_to)

    def wz_step(step):
        for way in (1, -1):
            c_wz[step, way].wait_recv()
            if step < NZ // 2:
                c_wz[step + 1, way] = wz(step + 1, way)

    loads["k"].wait()
    loads["v"].wait()
    fade = jnp.exp(within[TOK - 1:TOK, :] - within)
    for h in range(HEADS):
        lanes = slice(h * HD, (h + 1) * HD)
        kd = (k[:, lanes].astype(F32) * fade[:, h:h + 1]).astype(BF16)
        st[lanes, :] = dot(kd, v[:, lanes], TN).astype(BF16)
    c_st = [None]
    for i in range(1, GROUP):
        there = lax.rem(p + i, GROUP)
        part = st.at[pl.ds(pl.multiple_of(there * SLICE, SLICE), SLICE)]
        c_st.append(send(part, rs.at[p], group_dev[i]))
    rs[p] = st[pl.ds(pl.multiple_of(p * SLICE, SLICE), SLICE), :]

    wz_step(1)

    loads["q"].wait()
    for h in range(HEADS):
        lanes = slice(h * HD, (h + 1) * HD)
        spread = within[:, h:h + 1] - wrow[h:h + 1, :]
        factor = jnp.exp(jnp.where(lower, spread, -1e30))
        scores = dot(q[:, lanes], k[:, lanes], NT)
        intra[:, lanes] = dot((scores * factor).astype(BF16), v[:, lanes])

    wz_step(2)
    c_swap.wait_recv()
    own_kv = kvb.at[sz, sx, cc]
    c_kx = [send(own_kv, own_kv, cross_dev[i]) for i in range(1, NX)]

    for i in range(1, GROUP):
        c_dec[i].wait_recv()
        c_st[i].wait_recv()
    row = pl.ds(p // (GROUP // HEADS), 1)
    state = jnp.zeros((SLICE, HD), F32)
    passed = jnp.zeros((1, HD), F32)
    before = []
    for i in range(GROUP):
        ex[i] = state
        before.append(passed)
        step = dec[i, row, :]
        state = jnp.exp(step) * state + rs[i].astype(F32)
        passed = passed + step
    xs[sx, 0:SLICE, :] = state
    xs[sx, SLICE:SLICE + 8, :] = jnp.broadcast_to(passed, (8, HD))
    c_xs = [send(xs.at[sx], xs.at[sx], cross_dev[i]) for i in range(1, NX)]

    wz_step(3)

    for copy in c_xs:
        copy.wait_recv()
    base = jnp.zeros((SLICE, HD), F32)
    for x in range(NX - 1):
        fresh = jnp.exp(xs[x, SLICE:SLICE + 1, :]) * base + xs[x, 0:SLICE, :]
        base = jnp.where(x < sx, fresh, base)
    for i in range(GROUP):
        ob[i] = (ex[i] + jnp.exp(before[i]) * base).astype(BF16)
    c_inc = []
    for i in range(1, GROUP):
        c_inc.append(send(ob.at[lax.rem(p + i, GROUP)], inc.at[p], group_dev[i]))
    inc[p] = ob[p]

    wz_step(4)
    c_wx = {(1, way): wx(1, way) for way in (1, -1)}
    c_sib = [to_sibling(wbuf.at[sx, :, sc])]
    for copy in c_kx:
        copy.wait_recv()

    loads["g"].wait()
    loads["r"].wait()
    for copy in c_inc:
        copy.wait_recv()

    c_kz = {(1, way): kz(1, way) for way in (1, -1)}
    c_sib.append(to_sibling(kvb.at[sz, :, cc]))

    def kz_step(step):
        for way in (1, -1):
            c_kz[step, way].wait_recv()
            origin = lax.rem(sz - way * step + NZ, NZ)
            if step < NZ // 2:
                c_kz[step + 1, way] = kz(step + 1, way)
                c_sib.append(to_sibling(kvb.at[origin, :, cc]))
            else:
                half = pl.ds(0 if way == 1 else NX // 2, NX // 2)
                c_sib.append(to_sibling(kvb.at[origin, half, cc]))

    def wx_step(step):
        for way in (1, -1):
            c_wx[step, way].wait_recv()
            origin = lax.rem(sx - way * step + NX, NX)
            if step == 1:
                c_wx[2, way] = wx(2, way)
                c_sib.append(to_sibling(wbuf.at[origin, :, sc]))
            else:
                half = pl.ds(0 if way == 1 else NZ // 2, NZ // 2)
                c_sib.append(to_sibling(wbuf.at[origin, half, sc]))

    c_mix = {}

    def mix_send(step, way, chunk):
        origin = lax.rem(hy - way * (step - 1) + NY, NY)
        part = abuf.at[origin, pl.ds(chunk * MIX_ROWS, MIX_ROWS)]
        c_mix[step, way, chunk] = send(part, part, right_y if way == 1 else left_y)

    def goes(step, way, chunk):
        if step < NY // 2:
            return True
        return (chunk < MIX_CHUNKS // 2) == (way == 1)

    grown = jnp.exp(within)
    for chunk in range(MIX_CHUNKS):
        span = slice(chunk * MIX_ROWS, (chunk + 1) * MIX_ROWS)
        for h in range(HEADS):
            lanes = slice(h * HD, (h + 1) * HD)
            entering = inc[4 * h:4 * h + 4].reshape(HD, HD)
            kept = intra[span, lanes] + grown[span, h:h + 1] * dot(q[span, lanes], entering)
            scale = lax.rsqrt(jnp.mean(kept * kept, axis=1, keepdims=True) + 1e-6)
            opened = g[span, lanes].astype(F32)
            opened = opened / (1.0 + jnp.exp(-opened))
            abuf[hy, span, lanes] = (opened * (kept * scale)).astype(BF16)
        for way in (1, -1):
            mix_send(1, way, chunk)

    for step in range(1, NY // 2):
        for chunk in range(MIX_CHUNKS):
            for way in (1, -1):
                c_mix[step, way, chunk].wait_recv()
                if goes(step + 1, way, chunk):
                    mix_send(step + 1, way, chunk)
        kz_step(step)
        if step < 3:
            wx_step(step)

    for copy in c_sib:
        copy.wait_recv()

    def project(origin):
        weight = wbuf[origin // 2, pl.ds(lax.rem(origin, 2) * 4, 4)].reshape(WID, WID)
        acc[...] += dot(abuf[origin], weight)

    acc[...] = res[...].astype(F32)

    def projected(i, carry):
        project(lax.rem(hy - (NY // 2 - 1) + i + NY, NY))
        return carry

    lax.fori_loop(0, NY - 1, projected, 0)
    for chunk in range(MIX_CHUNKS):
        for way in (1, -1):
            if goes(NY // 2, way, chunk):
                c_mix[NY // 2, way, chunk].wait_recv()
    project(lax.rem(hy + NY // 2, NY))

    hidden = acc[...].astype(BF16).astype(F32)
    squares = jnp.sum(hidden * hidden, axis=1, keepdims=True)
    sq[hy] = jnp.transpose(jnp.broadcast_to(squares, (TOK, HD)))[0:8, :]
    c_sq = [send(sq.at[hy], sq.at[hy], head_dev[i]) for i in range(1, NY)]
    hg[...] = (hidden * gain_ref[...].astype(F32)).astype(BF16)

    known = len(c_sib)
    kz_step(4)
    for copy in c_sib[known:]:
        copy.wait_recv()

    def partial(origin, span):
        return dot(hg[span, :], kvb[origin].reshape(WID, 2 * HD))

    c_red = {}
    half = NY // 2
    for step in range(half):
        for late in (False, True):
            for chunk in range(RED_CHUNKS):
                span = slice(chunk * RED_ROWS, (chunk + 1) * RED_ROWS)
                for way in (1, -1):
                    far = (chunk < RED_CHUNKS // 2) == (way == 1)
                    if step == 0 and not far:
                        continue
                    joins = step > 1 or (step == 1 and far)
                    if joins != late:
                        continue
                    out, came = (sr, rr) if way == 1 else (sl, rl)
                    value = partial(lax.rem(hy + way * (half - step) + NY, NY), span)
                    if joins:
                        c_red[step - 1, way, chunk].wait_recv()
                        value = value + came[step - 1, span, :].astype(F32)
                    out[step, span, :] = value.astype(BF16)
                    c_red[step, way, chunk] = send(
                        out.at[step, pl.ds(chunk * RED_ROWS, RED_ROWS)],
                        came.at[step, pl.ds(chunk * RED_ROWS, RED_ROWS)],
                        right_y if way == 1 else left_y,
                    )
    for copy in c_sq:
        copy.wait_recv()
    total = sq[0]
    for y in range(1, NY):
        total = total + sq[y]
    inverse = jnp.transpose(lax.rsqrt(total / (WID * NY) + 1e-6))
    for chunk in range(RED_CHUNKS):
        span = slice(chunk * RED_ROWS, (chunk + 1) * RED_ROWS)
        value = partial(hy, span)
        for way, came in ((1, rr), (-1, rl)):
            c_red[half - 1, way, chunk].wait_recv()
            value = value + came[half - 1, span, :].astype(F32)
        value = (value * inverse[span, 0:1]).astype(BF16)
        ok_ref[span, :] = value[:, :HD]
        ov_ref[span, :] = value[:, HD:]
    drain()


def on_device(queries, keys, values, gate, residual, log_decay, out_weight, norm_gain, kv_weight):
    anywhere = pl.BlockSpec(memory_space=pl.ANY)
    vmem = pl.BlockSpec(memory_space=pltpu.VMEM)
    block = pltpu.VMEM((TOK, WID), BF16)
    out = jax.ShapeDtypeStruct((TOK, HD), BF16)
    reds = pltpu.VMEM((NY // 2, TOK, 2 * HD), BF16)
    return pl.pallas_call(
        layer_kernel,
        out_shape=(out, out),
        in_specs=[anywhere] * 5 + [vmem, anywhere, vmem, anywhere],
        out_specs=(vmem, vmem),
        scratch_shapes=[
            block, block, block, block, block,
            pltpu.VMEM((NX, NZ, NC, 64, WID), BF16),
            pltpu.VMEM((NZ, NX, NC, 64, 2 * HD), BF16),
            pltpu.VMEM((64, 2 * HD), BF16),
            pltpu.VMEM((TOK, 8), F32),
            pltpu.VMEM((HEADS * HD, HD), BF16),
            pltpu.VMEM((GROUP, SLICE, HD), BF16),
            pltpu.VMEM((GROUP, 8, HD), F32),
            pltpu.VMEM((NX, SLICE + 8, HD), F32),
            pltpu.VMEM((GROUP, SLICE, HD), F32),
            pltpu.VMEM((GROUP, SLICE, HD), BF16),
            pltpu.VMEM((GROUP, SLICE, HD), BF16),
            pltpu.VMEM((TOK, WID), F32),
            pltpu.VMEM((NY, TOK, WID), BF16),
            pltpu.VMEM((TOK, WID), F32),
            block,
            reds, reds, reds, reds,
            pltpu.VMEM((NY, 8, TOK), F32),
            pltpu.SemaphoreType.DMA((8,)),
            pltpu.SemaphoreType.DMA((COPIES,)),
            pltpu.SemaphoreType.DMA((COPIES,)),
        ],
        compiler_params=pltpu.CompilerParams(
            collective_id=0, has_side_effects=True, vmem_limit_bytes=40 << 20
        ),
    )(
        queries, keys, values, gate, residual, log_decay.T, out_weight,
        norm_gain.reshape(1, WID), kv_weight,
    )


def solution(mesh):
    placed = (P("seq", "head"),) * 7 + (P("head"), P("seq", "head"))
    return jax.shard_map(
        on_device,
        mesh=mesh,
        in_specs=placed,
        out_specs=(P("seq", "head"), P("seq", "head")),
        check_vma=False,
    )
```

```python
import functools

import jax
import jax.numpy as jnp
from jax import lax
from jax.experimental import pallas as pl
from jax.experimental.pallas import tpu as pltpu
from jax.sharding import PartitionSpec as P

MESH = pl.DeviceIdType.MESH
HIGHEST = lax.Precision.HIGHEST
F32, BF16 = jnp.float32, jnp.bfloat16

NX, NZ, NC, NY = 4, 8, 2, 8
GROUP = NZ * NC
TOK, WID, HEADS, HD = 256, 512, 4, 128
SLICE = HEADS * HD // GROUP
CHUNKS = 4
ROWS = TOK // CHUNKS
COPIES = 105
ORDER = (0, 2, 1, 3)


def dot(a, b, dims=(((1,), (0,)), ((), ())), precision=None):
    return lax.dot_general(a, b, dims, precision=precision, preferred_element_type=F32)


NT = (((1,), (1,)), ((), ()))
TN = (((0,), (0,)), ((), ()))


def layer_kernel(
    q_h, k_h, v_h, g_h, r_h, ld_ref, ow_h, gain_ref, kw_h,
    out_ref,
    q, k, v, g, res, wbuf, kvb, kin, st, rs, dsr, dec, xs, ex, ob, inc,
    intra, abuf, acc, hg, red_out, red_in, scol, sq,
    lsem, sem,
):
    seq, hy = lax.axis_index("seq"), lax.axis_index("head")
    sx, p = seq // GROUP, lax.rem(seq, GROUP)
    sz, sc = p // NC, lax.rem(p, NC)
    cc = 1 - sc

    def at(x, z, c, y):
        return (lax.rem(x + NX, NX) * GROUP + lax.rem(z + NZ, NZ) * NC + c, lax.rem(y + NY, NY))

    count = [0]

    def new_sem():
        count[0] += 1
        return sem.at[count[0] - 1]

    home = at(sx, sz, cc, hy)
    drains = []

    class Stream:
        def __init__(self, whole):
            self.sent = new_sem()
            drains.append((whole, self.sent))

        def send(self, src, dst, device, came):
            copy = pltpu.make_async_remote_copy(
                src_ref=src, dst_ref=dst, send_sem=self.sent, recv_sem=came,
                device_id=device, device_id_type=MESH,
            )
            copy.start()
            return copy

    def arrived(whole, came):
        pltpu.make_async_remote_copy(
            src_ref=whole, dst_ref=whole, send_sem=came, recv_sem=came,
            device_id=home, device_id_type=MESH,
        ).wait_recv()

    loads = {}
    for i, (name, src, dst) in enumerate((
        ("w", ow_h, wbuf.at[sx, sz, sc]), ("kw", kw_h, kin), ("k", k_h, k), ("v", v_h, v),
        ("q", q_h, q), ("g", g_h, g), ("r", r_h, res),
    )):
        loads[name] = pltpu.make_async_copy(src, dst, lsem.at[i])
        loads[name].start()

    swap_to = at(lax.rem(sz, NX), hy, cc, 2 * sx + sz // 4)
    swap_from = at(hy // 2, lax.rem(hy, 2) * 4 + sx, cc, sz)
    barrier = pltpu.get_barrier_semaphore()
    group = [lax.rem(p + i, GROUP) for i in range(GROUP)]
    group_dev = [(sx * GROUP + there, hy) for there in group]
    cross_dev = [at(sx + i, sz, sc, hy) for i in range(NX)]
    head_dev = [at(sx, sz, sc, hy + i) for i in range(NY)]
    greeted = group_dev[1:] + cross_dev[1:] + head_dev[1:] + [swap_to, swap_from]
    for device in greeted:
        pl.semaphore_signal(barrier, inc=1, device_id=device, device_id_type=MESH)

    rows = lax.broadcasted_iota(jnp.int32, (TOK, TOK), 0)
    cols = lax.broadcasted_iota(jnp.int32, (TOK, TOK), 1)
    lower = rows >= cols
    ld = jnp.concatenate([ld_ref[...], jnp.zeros((8 - HEADS, TOK), F32)], axis=0)
    wrow = dot(ld, (rows <= cols).astype(F32), precision=HIGHEST)
    within = dot(lower.astype(F32), ld, NT, precision=HIGHEST)
    for h in range(HEADS):
        dsr[h] = jnp.broadcast_to(wrow[h:h + 1, TOK - 1:TOK], (1, HD))

    pl.semaphore_wait(barrier, len(greeted))

    right_z, left_z = at(sx, sz + 1, sc, hy), at(sx, sz - 1, sc, hy)
    right_x, left_x = at(sx + 1, sz, sc, hy), at(sx - 1, sz, sc, hy)
    right_y, left_y = at(sx, sz, sc, hy + 1), at(sx, sz, sc, hy - 1)

    s_wz = Stream(wbuf.at[0, pl.ds(0, NZ - 1), 0])
    s_wx = Stream(wbuf.at[pl.ds(0, NX - 1), :, 0])
    s_wc = Stream(wbuf.at[:, :, 0])
    s_kz = Stream(kvb.at[pl.ds(0, NZ - 1), :, 0])
    s_kc = Stream(kvb.at[:, :, 0])
    wc_came, kc_came = new_sem(), new_sem()
    wx_came = {1: new_sem(), -1: new_sem()}

    def wz(step, way):
        origin = lax.rem(sz - way * (step - 1) + NZ, NZ)
        if step < NZ // 2:
            part = wbuf.at[sx, origin, sc]
        else:
            part = wbuf.at[sx, origin, sc, pl.ds(0 if way == 1 else 32, 32)]
        return s_wz.send(part, part, right_z if way == 1 else left_z, new_sem())

    def wx_first(origin):
        part = wbuf.at[sx, origin, sc]
        for way in (1, -1):
            s_wx.send(part, part, right_x if way == 1 else left_x, wx_came[way])

    def wx_second(way):
        part = wbuf.at[lax.rem(sx - way + NX, NX), pl.ds(0 if way == 1 else NZ // 2, NZ // 2), sc]
        return s_wx.send(part, part, right_x if way == 1 else left_x, new_sem())

    def kz(step, way, half):
        origin = lax.rem(sz - way * (step - 1) + NZ, NZ)
        part = kvb.at[origin, pl.ds(half * 2, 2), cc]
        return s_kz.send(part, part, right_z if way == 1 else left_z, new_sem())

    def w_sibling(part):
        s_wc.send(part, part, home, wc_came)

    def k_sibling(part):
        s_kc.send(part, part, home, kc_came)

    s_dec, dec_came = Stream(dec.at[pl.ds(0, GROUP - 1)]), new_sem()
    for i in range(1, GROUP):
        s_dec.send(dsr.at[group[i] // (GROUP // HEADS)], dec.at[p], group_dev[i], dec_came)
    dec[p] = dsr[p // (GROUP // HEADS)]
    loads["w"].wait()
    c_wz = {(1, way): wz(1, way) for way in (1, -1)}
    wx_first(sz)
    loads["kw"].wait()
    c_swap = Stream(kin).send(kin, kvb.at[hy, lax.rem(sz, NX), sc], swap_to, new_sem())

    def wz_step(step):
        for way in (1, -1):
            c_wz[step, way].wait_recv()
            if step < NZ // 2:
                c_wz[step + 1, way] = wz(step + 1, way)
        for way in (1, -1):
            if step < NZ // 2 or way == 1:
                wx_first(lax.rem(sz - way * step + NZ, NZ))

    loads["k"].wait()
    loads["v"].wait()
    fade = jnp.exp(within[TOK - 1:TOK, :] - within)
    for h in range(HEADS):
        lanes = slice(h * HD, (h + 1) * HD)
        kd = (k[:, lanes].astype(F32) * fade[:, h:h + 1]).astype(BF16)
        st[h * 4:h * 4 + 4] = dot(kd, v[:, lanes], TN).astype(BF16).reshape(4, SLICE, HD)
    s_st, st_came = Stream(rs.at[pl.ds(0, GROUP - 1)]), new_sem()
    for i in range(1, GROUP):
        s_st.send(st.at[group[i]], rs.at[p], group_dev[i], st_came)
    rs[p] = st[p]

    wz_step(1)

    loads["q"].wait()
    for h in range(HEADS):
        lanes = slice(h * HD, (h + 1) * HD)
        spread = within[:, h:h + 1] - wrow[h:h + 1, :]
        factor = jnp.exp(jnp.where(lower, spread, -1e30))
        scores = dot(q[:, lanes], k[:, lanes], NT)
        intra[:, lanes] = dot((scores * factor).astype(BF16), v[:, lanes])

    wz_step(2)
    c_swap.wait_recv()
    own_kv = kvb.at[sz, sx, cc]
    s_kx, kx_came = Stream(kvb.at[0, pl.ds(0, NX - 1), 0]), new_sem()
    for i in range(1, NX):
        s_kx.send(own_kv, own_kv, cross_dev[i], kx_came)

    arrived(dec.at[pl.ds(0, GROUP - 1)], dec_came)
    arrived(rs.at[pl.ds(0, GROUP - 1)], st_came)
    state = jnp.zeros((SLICE, HD), F32)
    passed = jnp.zeros((1, HD), F32)
    before = []
    for i in range(GROUP):
        ex[i] = state
        before.append(passed)
        step = dec[i]
        state = jnp.exp(step) * state + rs[i].astype(F32)
        passed = passed + step
    xs[sx, 0:SLICE, :] = state
    xs[sx, SLICE:SLICE + 8, :] = jnp.broadcast_to(passed, (8, HD))
    s_xs, xs_came = Stream(xs.at[pl.ds(0, NX - 1)]), new_sem()
    for i in range(1, NX):
        s_xs.send(xs.at[sx], xs.at[sx], cross_dev[i], xs_came)

    wz_step(3)

    arrived(xs.at[pl.ds(0, NX - 1)], xs_came)
    base = jnp.zeros((SLICE, HD), F32)
    for x in range(NX - 1):
        fresh = jnp.exp(xs[x, SLICE:SLICE + 1, :]) * base + xs[x, 0:SLICE, :]
        base = jnp.where(x < sx, fresh, base)
    for i in range(GROUP):
        ob[i] = (ex[i] + jnp.exp(before[i]) * base).astype(BF16)
    s_inc, inc_came = Stream(ob.at[pl.ds(0, GROUP - 1)]), new_sem()
    for i in range(1, GROUP):
        s_inc.send(ob.at[group[i]], inc.at[p], group_dev[i], inc_came)
    inc[p] = ob[p]

    wz_step(4)
    w_sibling(wbuf.at[sx, :, sc])
    loads["g"].wait()
    loads["r"].wait()
    arrived(kvb.at[0, pl.ds(0, NX - 1), 0], kx_came)
    arrived(inc.at[pl.ds(0, GROUP - 1)], inc_came)

    c_kz = {(1, way, half): kz(1, way, half) for half in (0, 1) for way in (1, -1)}
    k_sibling(kvb.at[sz, :, cc])
    c_wx = {}

    def kz_step(step, half):
        for way in (1, -1):
            if (step, way, half) not in c_kz:
                continue
            c_kz[step, way, half].wait_recv()
            if step + 1 < NZ // 2 or (step + 1 == NZ // 2 and half == (0 if way == 1 else 1)):
                c_kz[step + 1, way, half] = kz(step + 1, way, half)
            origin = lax.rem(sz - way * step + NZ, NZ)
            k_sibling(kvb.at[origin, pl.ds(half * 2, 2), cc])

    def wx_step(step):
        for way in (1, -1):
            origin = lax.rem(sx - way * step + NX, NX)
            if step == 1:
                arrived(wbuf.at[0, :, 0], wx_came[way])
                c_wx[way] = wx_second(way)
                w_sibling(wbuf.at[origin, :, sc])
            else:
                c_wx[way].wait_recv()
                half = pl.ds(0 if way == 1 else NZ // 2, NZ // 2)
                w_sibling(wbuf.at[origin, half, sc])

    s_mix, c_mix = Stream(abuf.at[pl.ds(0, NY - 1)]), {}

    def far(chunk):
        return 1 if chunk < CHUNKS // 2 else -1

    def mix_send(step, way, chunk):
        if step == NY // 2 and way != far(chunk):
            return
        origin = lax.rem(hy - way * (step - 1) + NY, NY)
        part = abuf.at[origin, pl.ds(chunk * ROWS, ROWS)]
        c_mix[step, way, chunk] = s_mix.send(part, part, right_y if way == 1 else left_y, new_sem())

    grown = jnp.exp(within)
    for chunk in ORDER:
        span = slice(chunk * ROWS, (chunk + 1) * ROWS)
        for h in range(HEADS):
            lanes = slice(h * HD, (h + 1) * HD)
            entering = inc[4 * h:4 * h + 4].reshape(HD, HD)
            kept = intra[span, lanes] + grown[span, h:h + 1] * dot(q[span, lanes], entering)
            scale = lax.rsqrt(jnp.mean(kept * kept, axis=1, keepdims=True) + 1e-6)
            opened = g[span, lanes].astype(F32)
            opened = opened / (1.0 + jnp.exp(-opened))
            abuf[hy, span, lanes] = (opened * (kept * scale)).astype(BF16)
        for way in (1, -1):
            mix_send(1, way, chunk)

    service = {
        0: (lambda: wx_step(1),),
        1: (lambda: kz_step(1, 0),), 2: (lambda: kz_step(1, 1),),
        4: (lambda: kz_step(2, 0),), 5: (lambda: kz_step(2, 1),),
        6: (lambda: wx_step(2),),
        7: (lambda: kz_step(3, 0),), 8: (lambda: kz_step(3, 1),),
        10: (lambda: kz_step(4, 0), lambda: kz_step(4, 1)),
    }
    for step in range(1, NY // 2):
        for n, chunk in enumerate(ORDER):
            for way in (1, -1):
                c_mix[step, way, chunk].wait_recv()
                mix_send(step + 1, way, chunk)
            for job in service.get((step - 1) * CHUNKS + n, ()):
                job()

    arrived(wbuf.at[:, :, 0], wc_came)

    def weight(origin):
        return wbuf[origin // 2, pl.ds(lax.rem(origin, 2) * 4, 4)].reshape(WID, WID)

    acc[...] = res[...].astype(F32)

    def projected(i, carry):
        origin = lax.rem(hy - (NY // 2 - 1) + i + NY, NY)
        acc[...] += dot(abuf[origin], weight(origin))
        return carry

    lax.fori_loop(0, NY - 1, projected, 0)
    arrived(kvb.at[:, :, 0], kc_came)

    last = lax.rem(hy + NY // 2, NY)
    s_red, c_red = Stream(red_out.at[pl.ds(0, NY - 1)]), {}

    def reduce_send(step, way, chunk):
        span = slice(chunk * ROWS, (chunk + 1) * ROWS)
        slot = step * 2 + (0 if way == 1 else 1)
        origin = lax.rem(hy + way * (NY // 2 - step) + NY, NY)
        value = dot(hg[span, :], kvb[origin].reshape(WID, 2 * HD))
        if (step - 1, way, chunk) in c_red:
            c_red[step - 1, way, chunk].wait_recv()
            value = value + red_in[slot - 2, span, :].astype(F32)
        red_out[slot, span, :] = value.astype(BF16)
        c_red[step, way, chunk] = s_red.send(
            red_out.at[slot, pl.ds(chunk * ROWS, ROWS)], red_in.at[slot, pl.ds(chunk * ROWS, ROWS)],
            right_y if way == 1 else left_y, new_sem(),
        )

    gain = gain_ref[...].astype(F32).reshape(1, WID)
    for chunk in ORDER:
        span = slice(chunk * ROWS, (chunk + 1) * ROWS)
        c_mix[NY // 2, far(chunk), chunk].wait_recv()
        hidden = (acc[span, :] + dot(abuf[last, span, :], weight(last))).astype(BF16).astype(F32)
        hg[span, :] = (hidden * gain).astype(BF16)
        scol[span, :] = jnp.broadcast_to(jnp.sum(hidden * hidden, axis=1, keepdims=True), (ROWS, HD))
        reduce_send(0, far(chunk), chunk)
        reduce_send(1, -far(chunk), chunk)
    sq[hy] = jnp.transpose(scol[...])[0:8, :]
    s_sq, sq_came = Stream(sq.at[pl.ds(0, NY - 1)]), new_sem()
    for i in range(1, NY):
        s_sq.send(sq.at[hy], sq.at[hy], head_dev[i], sq_came)
    for chunk in ORDER:
        reduce_send(1, far(chunk), chunk)
    for step in range(2, NY // 2):
        for late in (False, True):
            for chunk in ORDER:
                reduce_send(step, far(chunk) if late else -far(chunk), chunk)
    arrived(sq.at[pl.ds(0, NY - 1)], sq_came)
    total = sq[0]
    for y in range(1, NY):
        total = total + sq[y]
    inverse = jnp.transpose(lax.rsqrt(total / (WID * NY) + 1e-6))
    for chunk in ORDER:
        span = slice(chunk * ROWS, (chunk + 1) * ROWS)
        value = dot(hg[span, :], kvb[hy].reshape(WID, 2 * HD))
        for way in (1, -1):
            c_red[NY // 2 - 1, way, chunk].wait_recv()
            slot = NY - 2 + (0 if way == 1 else 1)
            value = value + red_in[slot, span, :].astype(F32)
        out_ref[span, :] = (value * inverse[span, 0:1]).astype(BF16)

    assert count[0] <= COPIES, count[0]
    for whole, sent in drains:
        pltpu.make_async_remote_copy(
            src_ref=whole, dst_ref=whole, send_sem=sent, recv_sem=sent,
            device_id=home, device_id_type=MESH,
        ).wait_send()


def on_device(queries, keys, values, gate, residual, log_decay, out_weight, norm_gain, kv_weight):
    hbm = pl.BlockSpec(memory_space=pltpu.HBM)
    vmem = pl.BlockSpec(memory_space=pltpu.VMEM)
    block = pltpu.VMEM((TOK, WID), BF16)
    reds = pltpu.VMEM((NY, TOK, 2 * HD), BF16)
    slices = pltpu.VMEM((GROUP, SLICE, HD), BF16)
    both = pl.pallas_call(
        layer_kernel,
        out_shape=jax.ShapeDtypeStruct((TOK, 2 * HD), BF16),
        in_specs=[hbm] * 5 + [vmem, hbm, vmem, hbm],
        out_specs=vmem,
        scratch_shapes=[
            block, block, block, block, block,
            pltpu.VMEM((NX, NZ, NC, 64, WID), BF16),
            pltpu.VMEM((NZ, NX, NC, 64, 2 * HD), BF16),
            pltpu.VMEM((64, 2 * HD), BF16),
            slices,
            slices,
            pltpu.VMEM((HEADS, 1, HD), F32),
            pltpu.VMEM((GROUP, 1, HD), F32),
            pltpu.VMEM((NX, SLICE + 8, HD), F32),
            pltpu.VMEM((GROUP, SLICE, HD), F32),
            slices,
            slices,
            pltpu.VMEM((TOK, WID), F32),
            pltpu.VMEM((NY, TOK, WID), BF16),
            pltpu.VMEM((TOK, WID), F32),
            block,
            reds, reds,
            pltpu.VMEM((TOK, HD), F32),
            pltpu.VMEM((NY, 8, TOK), F32),
            pltpu.SemaphoreType.DMA((7,)),
            pltpu.SemaphoreType.DMA((COPIES,)),
        ],
        compiler_params=pltpu.CompilerParams(
            collective_id=0, has_side_effects=True, vmem_limit_bytes=62 << 20
        ),
    )(
        queries, keys, values, gate, residual, log_decay.T, out_weight, norm_gain, kv_weight,
    )
    return both[:, :HD], both[:, HD:]


def solution(mesh):
    placed = (P("seq", "head"),) * 7 + (P("head"), P("seq", "head"))
    return jax.shard_map(
        on_device,
        mesh=mesh,
        in_specs=placed,
        out_specs=(P("seq", "head"), P("seq", "head")),
        check_vma=False,
    )
```

```python
import functools

import jax
import jax.numpy as jnp
from jax import lax
from jax.experimental import pallas as pl
from jax.experimental.pallas import tpu as pltpu
from jax.sharding import PartitionSpec as P

MESH = pl.DeviceIdType.MESH
HIGHEST = lax.Precision.HIGHEST
F32, BF16 = jnp.float32, jnp.bfloat16

NX, NZ, NC, NY = 4, 8, 2, 8
GROUP = NZ * NC
TOK, WID, HEADS, HD = 256, 512, 4, 128
SLICE = HEADS * HD // GROUP
CHUNKS = 4
ROWS = TOK // CHUNKS
COPIES = 105
ORDER = (0, 2, 1, 3)


def dot(a, b, dims=(((1,), (0,)), ((), ())), precision=None):
    return lax.dot_general(a, b, dims, precision=precision, preferred_element_type=F32)


NT = (((1,), (1,)), ((), ()))
TN = (((0,), (0,)), ((), ()))


def layer_kernel(
    q_h, k_h, v_h, g_h, r_h, ld_ref, ow_h, gain_ref, kw_h,
    out_ref,
    q, k, v, g, res, wbuf, kvb, kin, st, rs, dsr, dec, xs, ex, ob, inc,
    intra, abuf, acc, hg, red_out, red_in, scol, sq,
    lsem, sem,
):
    seq, hy = lax.axis_index("seq"), lax.axis_index("head")
    sx, p = seq // GROUP, lax.rem(seq, GROUP)
    sz, sc = p // NC, lax.rem(p, NC)
    cc = 1 - sc

    def at(x, z, c, y):
        return (lax.rem(x + NX, NX) * GROUP + lax.rem(z + NZ, NZ) * NC + c, lax.rem(y + NY, NY))

    count = [0]

    def new_sem():
        count[0] += 1
        return sem.at[count[0] - 1]

    home = at(sx, sz, cc, hy)
    drains = []

    class Stream:
        def __init__(self, whole):
            self.sent = new_sem()
            drains.append((whole, self.sent))

        def send(self, src, dst, device, came):
            copy = pltpu.make_async_remote_copy(
                src_ref=src, dst_ref=dst, send_sem=self.sent, recv_sem=came,
                device_id=device, device_id_type=MESH,
            )
            copy.start()
            return copy

    def arrived(whole, came):
        pltpu.make_async_remote_copy(
            src_ref=whole, dst_ref=whole, send_sem=came, recv_sem=came,
            device_id=home, device_id_type=MESH,
        ).wait_recv()

    loads = {}
    for i, (name, src, dst) in enumerate((
        ("w", ow_h, wbuf.at[sx, sz, sc]), ("kw", kw_h, kin), ("k", k_h, k), ("v", v_h, v),
        ("q", q_h, q), ("g", g_h, g), ("r", r_h, res),
    )):
        loads[name] = pltpu.make_async_copy(src, dst, lsem.at[i])
        loads[name].start()

    swap_to = at(lax.rem(sz, NX), hy, cc, 2 * sx + sz // 4)
    swap_from = at(hy // 2, lax.rem(hy, 2) * 4 + sx, cc, sz)
    barrier = pltpu.get_barrier_semaphore()
    group = [lax.rem(p + i, GROUP) for i in range(GROUP)]
    group_dev = [(sx * GROUP + there, hy) for there in group]
    cross_dev = [at(sx + i, sz, sc, hy) for i in range(NX)]
    head_dev = [at(sx, sz, sc, hy + i) for i in range(NY)]
    greeted = group_dev[1:] + cross_dev[1:] + head_dev[1:] + [swap_to, swap_from]
    for device in greeted:
        pl.semaphore_signal(barrier, inc=1, device_id=device, device_id_type=MESH)

    rows = lax.broadcasted_iota(jnp.int32, (TOK, TOK), 0)
    cols = lax.broadcasted_iota(jnp.int32, (TOK, TOK), 1)
    lower = rows >= cols
    ld = jnp.concatenate([ld_ref[...], jnp.zeros((8 - HEADS, TOK), F32)], axis=0)
    wrow = dot(ld, (rows <= cols).astype(F32), precision=HIGHEST)
    within = dot(lower.astype(F32), ld, NT, precision=HIGHEST)
    for h in range(HEADS):
        dsr[h] = jnp.broadcast_to(wrow[h:h + 1, TOK - 1:TOK], (1, HD))

    loads["k"].wait()
    loads["v"].wait()
    fade = jnp.exp(within[TOK - 1:TOK, :] - within)
    for h in range(HEADS):
        lanes = slice(h * HD, (h + 1) * HD)
        kd = (k[:, lanes].astype(F32) * fade[:, h:h + 1]).astype(BF16)
        st[h * 4:h * 4 + 4] = dot(kd, v[:, lanes], TN).astype(BF16).reshape(4, SLICE, HD)

    pl.semaphore_wait(barrier, len(greeted))

    right_z, left_z = at(sx, sz + 1, sc, hy), at(sx, sz - 1, sc, hy)
    right_x, left_x = at(sx + 1, sz, sc, hy), at(sx - 1, sz, sc, hy)
    right_y, left_y = at(sx, sz, sc, hy + 1), at(sx, sz, sc, hy - 1)

    s_wz = Stream(wbuf.at[0, pl.ds(0, NZ - 1), 0])
    s_wx = Stream(wbuf.at[pl.ds(0, NX - 1), :, 0])
    s_wc = Stream(wbuf.at[:, :, 0])
    s_kz = Stream(kvb.at[pl.ds(0, NZ - 1), :, 0])
    s_kc = Stream(kvb.at[:, :, 0])
    wc_came, kc_came = new_sem(), new_sem()
    wx_came = {1: new_sem(), -1: new_sem()}

    def wz(step, way):
        origin = lax.rem(sz - way * (step - 1) + NZ, NZ)
        if step < NZ // 2:
            part = wbuf.at[sx, origin, sc]
        else:
            part = wbuf.at[sx, origin, sc, pl.ds(0 if way == 1 else 32, 32)]
        return s_wz.send(part, part, right_z if way == 1 else left_z, new_sem())

    def wx_first(origin):
        part = wbuf.at[sx, origin, sc]
        for way in (1, -1):
            s_wx.send(part, part, right_x if way == 1 else left_x, wx_came[way])

    def wx_second(way):
        part = wbuf.at[lax.rem(sx - way + NX, NX), pl.ds(0 if way == 1 else NZ // 2, NZ // 2), sc]
        return s_wx.send(part, part, right_x if way == 1 else left_x, new_sem())

    def kz(step, way, half):
        origin = lax.rem(sz - way * (step - 1) + NZ, NZ)
        part = kvb.at[origin, pl.ds(half * 2, 2), cc]
        return s_kz.send(part, part, right_z if way == 1 else left_z, new_sem())

    def w_sibling(part):
        s_wc.send(part, part, home, wc_came)

    def k_sibling(part):
        s_kc.send(part, part, home, kc_came)

    s_dec, dec_came = Stream(dec.at[pl.ds(0, GROUP - 1)]), new_sem()
    for i in range(1, GROUP):
        s_dec.send(dsr.at[group[i] // (GROUP // HEADS)], dec.at[p], group_dev[i], dec_came)
    dec[p] = dsr[p // (GROUP // HEADS)]
    s_st, st_came = Stream(rs.at[pl.ds(0, GROUP - 1)]), new_sem()
    for i in range(1, GROUP):
        s_st.send(st.at[group[i]], rs.at[p], group_dev[i], st_came)
    rs[p] = st[p]

    loads["w"].wait()
    c_wz = {(1, way): wz(1, way) for way in (1, -1)}
    loads["kw"].wait()
    c_swap = Stream(kin).send(kin, kvb.at[hy, lax.rem(sz, NX), sc], swap_to, new_sem())

    def wz_step(step):
        for way in (1, -1):
            c_wz[step, way].wait_recv()
            if step < NZ // 2:
                c_wz[step + 1, way] = wz(step + 1, way)
    loads["q"].wait()
    for h in range(HEADS):
        lanes = slice(h * HD, (h + 1) * HD)
        spread = within[:, h:h + 1] - wrow[h:h + 1, :]
        factor = jnp.exp(jnp.where(lower, spread, -1e30))
        scores = dot(q[:, lanes], k[:, lanes], NT)
        intra[:, lanes] = dot((scores * factor).astype(BF16), v[:, lanes])

    wz_step(1)

    arrived(dec.at[pl.ds(0, GROUP - 1)], dec_came)
    arrived(rs.at[pl.ds(0, GROUP - 1)], st_came)
    state = jnp.zeros((SLICE, HD), F32)
    passed = jnp.zeros((1, HD), F32)
    before = []
    for i in range(GROUP):
        ex[i] = state
        before.append(passed)
        step = dec[i]
        state = jnp.exp(step) * state + rs[i].astype(F32)
        passed = passed + step
    xs[sx, 0:SLICE, :] = state
    xs[sx, SLICE:SLICE + 8, :] = jnp.broadcast_to(passed, (8, HD))
    s_xs, xs_came = Stream(xs.at[pl.ds(0, NX - 1)]), new_sem()
    for i in range(1, NX):
        s_xs.send(xs.at[sx], xs.at[sx], cross_dev[i], xs_came)

    wz_step(2)

    arrived(xs.at[pl.ds(0, NX - 1)], xs_came)
    base = jnp.zeros((SLICE, HD), F32)
    for x in range(NX - 1):
        fresh = jnp.exp(xs[x, SLICE:SLICE + 1, :]) * base + xs[x, 0:SLICE, :]
        base = jnp.where(x < sx, fresh, base)
    for i in range(GROUP):
        ob[i] = (ex[i] + jnp.exp(before[i]) * base).astype(BF16)
    s_inc, inc_came = Stream(ob.at[pl.ds(0, GROUP - 1)]), new_sem()
    for i in range(1, GROUP):
        s_inc.send(ob.at[group[i]], inc.at[p], group_dev[i], inc_came)
    inc[p] = ob[p]

    c_swap.wait_recv()
    own_kv = kvb.at[sz, sx, cc]
    s_kx, kx_came = Stream(kvb.at[0, pl.ds(0, NX - 1), 0]), new_sem()
    for i in range(1, NX):
        s_kx.send(own_kv, own_kv, cross_dev[i], kx_came)
    for step in (0, -1, 1, -2, 2):
        wx_first(lax.rem(sz + step + NZ, NZ))
    wz_step(3)
    for step in (-3, 3):
        wx_first(lax.rem(sz + step + NZ, NZ))
    wz_step(4)
    wx_first(lax.rem(sz + NZ // 2, NZ))
    w_sibling(wbuf.at[sx, :, sc])
    loads["g"].wait()
    loads["r"].wait()
    arrived(kvb.at[0, pl.ds(0, NX - 1), 0], kx_came)
    arrived(inc.at[pl.ds(0, GROUP - 1)], inc_came)

    c_kz = {(1, way, half): kz(1, way, half) for half in (0, 1) for way in (1, -1)}
    k_sibling(kvb.at[sz, :, cc])
    c_wx = {}

    def kz_step(step, half):
        for way in (1, -1):
            if (step, way, half) not in c_kz:
                continue
            c_kz[step, way, half].wait_recv()
            if step + 1 < NZ // 2 or (step + 1 == NZ // 2 and half == (0 if way == 1 else 1)):
                c_kz[step + 1, way, half] = kz(step + 1, way, half)
            origin = lax.rem(sz - way * step + NZ, NZ)
            k_sibling(kvb.at[origin, pl.ds(half * 2, 2), cc])

    def wx_step(step):
        for way in (1, -1):
            origin = lax.rem(sx - way * step + NX, NX)
            if step == 1:
                arrived(wbuf.at[0, :, 0], wx_came[way])
                c_wx[way] = wx_second(way)
                w_sibling(wbuf.at[origin, :, sc])
            else:
                c_wx[way].wait_recv()
                half = pl.ds(0 if way == 1 else NZ // 2, NZ // 2)
                w_sibling(wbuf.at[origin, half, sc])

    s_mix, c_mix = Stream(abuf.at[pl.ds(0, NY - 1)]), {}

    def far(chunk):
        return 1 if chunk < CHUNKS // 2 else -1

    def mix_send(step, way, chunk):
        if step == NY // 2 and way != far(chunk):
            return
        origin = lax.rem(hy - way * (step - 1) + NY, NY)
        part = abuf.at[origin, pl.ds(chunk * ROWS, ROWS)]
        c_mix[step, way, chunk] = s_mix.send(part, part, right_y if way == 1 else left_y, new_sem())

    grown = jnp.exp(within)
    for chunk in ORDER:
        span = slice(chunk * ROWS, (chunk + 1) * ROWS)
        for h in range(HEADS):
            lanes = slice(h * HD, (h + 1) * HD)
            entering = inc[4 * h:4 * h + 4].reshape(HD, HD)
            kept = intra[span, lanes] + grown[span, h:h + 1] * dot(q[span, lanes], entering)
            scale = lax.rsqrt(jnp.mean(kept * kept, axis=1, keepdims=True) + 1e-6)
            opened = g[span, lanes].astype(F32)
            opened = opened / (1.0 + jnp.exp(-opened))
            abuf[hy, span, lanes] = (opened * (kept * scale)).astype(BF16)
        for way in (1, -1):
            mix_send(1, way, chunk)

    service = {
        0: (lambda: kz_step(1, 0),), 1: (lambda: kz_step(1, 1),),
        2: (lambda: wx_step(1),),
        3: (lambda: kz_step(2, 0),), 4: (lambda: kz_step(2, 1),),
        6: (lambda: kz_step(3, 0),), 7: (lambda: kz_step(3, 1),),
        8: (lambda: wx_step(2),),
        9: (lambda: kz_step(4, 0), lambda: kz_step(4, 1)),
    }
    for step in range(1, NY // 2):
        for n, chunk in enumerate(ORDER):
            for way in (1, -1):
                c_mix[step, way, chunk].wait_recv()
                mix_send(step + 1, way, chunk)
            for job in service.get((step - 1) * CHUNKS + n, ()):
                job()

    arrived(wbuf.at[:, :, 0], wc_came)

    def weight(origin):
        return wbuf[origin // 2, pl.ds(lax.rem(origin, 2) * 4, 4)].reshape(WID, WID)

    acc[...] = res[...].astype(F32)

    def projected(i, carry):
        origin = lax.rem(hy - (NY // 2 - 1) + i + NY, NY)
        acc[...] += dot(abuf[origin], weight(origin))
        return carry

    lax.fori_loop(0, NY - 1, projected, 0)
    arrived(kvb.at[:, :, 0], kc_came)

    last = lax.rem(hy + NY // 2, NY)
    s_red, c_red = Stream(red_out.at[pl.ds(0, NY - 1)]), {}

    def reduce_send(step, way, chunk):
        span = slice(chunk * ROWS, (chunk + 1) * ROWS)
        slot = step * 2 + (0 if way == 1 else 1)
        origin = lax.rem(hy + way * (NY // 2 - step) + NY, NY)
        value = dot(hg[span, :], kvb[origin].reshape(WID, 2 * HD))
        if (step - 1, way, chunk) in c_red:
            c_red[step - 1, way, chunk].wait_recv()
            value = value + red_in[slot - 2, span, :].astype(F32)
        red_out[slot, span, :] = value.astype(BF16)
        c_red[step, way, chunk] = s_red.send(
            red_out.at[slot, pl.ds(chunk * ROWS, ROWS)], red_in.at[slot, pl.ds(chunk * ROWS, ROWS)],
            right_y if way == 1 else left_y, new_sem(),
        )

    gain = gain_ref[...].astype(F32).reshape(1, WID)
    for chunk in ORDER:
        span = slice(chunk * ROWS, (chunk + 1) * ROWS)
        c_mix[NY // 2, far(chunk), chunk].wait_recv()
        hidden = (acc[span, :] + dot(abuf[last, span, :], weight(last))).astype(BF16).astype(F32)
        hg[span, :] = (hidden * gain).astype(BF16)
        scol[span, :] = jnp.broadcast_to(jnp.sum(hidden * hidden, axis=1, keepdims=True), (ROWS, HD))
        reduce_send(0, far(chunk), chunk)
        reduce_send(1, -far(chunk), chunk)
    sq[hy] = jnp.transpose(scol[...])[0:8, :]
    s_sq, sq_came = Stream(sq.at[pl.ds(0, NY - 1)]), new_sem()
    for i in range(1, NY):
        s_sq.send(sq.at[hy], sq.at[hy], head_dev[i], sq_came)
    for chunk in ORDER:
        reduce_send(1, far(chunk), chunk)
    for step in range(2, NY // 2):
        for late in (False, True):
            for chunk in ORDER:
                reduce_send(step, far(chunk) if late else -far(chunk), chunk)
    arrived(sq.at[pl.ds(0, NY - 1)], sq_came)
    total = sq[0]
    for y in range(1, NY):
        total = total + sq[y]
    inverse = jnp.transpose(lax.rsqrt(total / (WID * NY) + 1e-6))
    for chunk in ORDER:
        span = slice(chunk * ROWS, (chunk + 1) * ROWS)
        value = dot(hg[span, :], kvb[hy].reshape(WID, 2 * HD))
        for way in (1, -1):
            c_red[NY // 2 - 1, way, chunk].wait_recv()
            slot = NY - 2 + (0 if way == 1 else 1)
            value = value + red_in[slot, span, :].astype(F32)
        out_ref[span, :] = (value * inverse[span, 0:1]).astype(BF16)

    assert count[0] <= COPIES, count[0]
    for whole, sent in drains:
        pltpu.make_async_remote_copy(
            src_ref=whole, dst_ref=whole, send_sem=sent, recv_sem=sent,
            device_id=home, device_id_type=MESH,
        ).wait_send()


def on_device(queries, keys, values, gate, residual, log_decay, out_weight, norm_gain, kv_weight):
    hbm = pl.BlockSpec(memory_space=pltpu.HBM)
    vmem = pl.BlockSpec(memory_space=pltpu.VMEM)
    block = pltpu.VMEM((TOK, WID), BF16)
    reds = pltpu.VMEM((NY, TOK, 2 * HD), BF16)
    slices = pltpu.VMEM((GROUP, SLICE, HD), BF16)
    both = pl.pallas_call(
        layer_kernel,
        out_shape=jax.ShapeDtypeStruct((TOK, 2 * HD), BF16),
        in_specs=[hbm] * 5 + [vmem, hbm, vmem, hbm],
        out_specs=vmem,
        scratch_shapes=[
            block, block, block, block, block,
            pltpu.VMEM((NX, NZ, NC, 64, WID), BF16),
            pltpu.VMEM((NZ, NX, NC, 64, 2 * HD), BF16),
            pltpu.VMEM((64, 2 * HD), BF16),
            slices,
            slices,
            pltpu.VMEM((HEADS, 1, HD), F32),
            pltpu.VMEM((GROUP, 1, HD), F32),
            pltpu.VMEM((NX, SLICE + 8, HD), F32),
            pltpu.VMEM((GROUP, SLICE, HD), F32),
            slices,
            slices,
            pltpu.VMEM((TOK, WID), F32),
            pltpu.VMEM((NY, TOK, WID), BF16),
            pltpu.VMEM((TOK, WID), F32),
            block,
            reds, reds,
            pltpu.VMEM((TOK, HD), F32),
            pltpu.VMEM((NY, 8, TOK), F32),
            pltpu.SemaphoreType.DMA((7,)),
            pltpu.SemaphoreType.DMA((COPIES,)),
        ],
        compiler_params=pltpu.CompilerParams(
            collective_id=0, has_side_effects=True, vmem_limit_bytes=62 << 20
        ),
    )(
        queries, keys, values, gate, residual, log_decay.T, out_weight, norm_gain, kv_weight,
    )
    return both[:, :HD], both[:, HD:]


def solution(mesh):
    placed = (P("seq", "head"),) * 7 + (P("head"), P("seq", "head"))
    return jax.shard_map(
        on_device,
        mesh=mesh,
        in_specs=placed,
        out_specs=(P("seq", "head"), P("seq", "head")),
        check_vma=False,
    )
```

```python
import functools

import jax
import jax.numpy as jnp
from jax import lax
from jax.experimental import pallas as pl
from jax.experimental.pallas import tpu as pltpu
from jax.sharding import PartitionSpec as P

MESH = pl.DeviceIdType.MESH
HIGHEST = lax.Precision.HIGHEST
F32, BF16 = jnp.float32, jnp.bfloat16

NX, NZ, NC, NY = 4, 8, 2, 8
GROUP = NZ * NC
TOK, WID, HEADS, HD = 256, 512, 4, 128
SLICE = HEADS * HD // GROUP
CHUNKS = 4
ROWS = TOK // CHUNKS
COPIES = 105
ORDER = (0, 2, 1, 3)


def dot(a, b, dims=(((1,), (0,)), ((), ())), precision=None):
    return lax.dot_general(a, b, dims, precision=precision, preferred_element_type=F32)


NT = (((1,), (1,)), ((), ()))
TN = (((0,), (0,)), ((), ()))


def layer_kernel(
    q_h, k_h, v_h, g_h, r_h, ld_ref, ow_h, gain_ref, kw_h,
    out_ref,
    q, k, v, g, res, wbuf, kvb, kin, st, rs, dsr, dec, xs, ex, ob, inc,
    intra, abuf, acc, hg, red_out, red_in, scol, sq,
    lsem, sem,
):
    seq, hy = lax.axis_index("seq"), lax.axis_index("head")
    sx, p = seq // GROUP, lax.rem(seq, GROUP)
    sz, sc = p // NC, lax.rem(p, NC)
    cc = 1 - sc

    def at(x, z, c, y):
        return (lax.rem(x + NX, NX) * GROUP + lax.rem(z + NZ, NZ) * NC + c, lax.rem(y + NY, NY))

    count = [0]

    def new_sem():
        count[0] += 1
        return sem.at[count[0] - 1]

    home = at(sx, sz, cc, hy)
    drains = []

    class Stream:
        def __init__(self, whole):
            self.sent = new_sem()
            drains.append((whole, self.sent))

        def send(self, src, dst, device, came):
            copy = pltpu.make_async_remote_copy(
                src_ref=src, dst_ref=dst, send_sem=self.sent, recv_sem=came,
                device_id=device, device_id_type=MESH,
            )
            copy.start()
            return copy

    def arrived(whole, came):
        pltpu.make_async_remote_copy(
            src_ref=whole, dst_ref=whole, send_sem=came, recv_sem=came,
            device_id=home, device_id_type=MESH,
        ).wait_recv()

    loads = {}
    for i, (name, src, dst) in enumerate((
        ("w", ow_h, wbuf.at[sx, sz, sc]), ("kw", kw_h, kin), ("k", k_h, k), ("v", v_h, v),
        ("q", q_h, q), ("g", g_h, g), ("r", r_h, res),
    )):
        loads[name] = pltpu.make_async_copy(src, dst, lsem.at[i])
        loads[name].start()

    swap_x, swap_z = lax.rem(hy, NX), jnp.where(hy < NX, sz, NZ - 1 - sz)
    swap_to = at(swap_x, swap_z, cc, 2 * sx + sz // 4)

    def kslot(z):
        return jnp.where((z // 4) != lax.rem(hy, 2), NZ - 1 - lax.rem(z, 4), lax.rem(z, 4))

    moved = (sz // 4) != lax.rem(hy, 2)
    swap_from = at(hy // 2, jnp.where(moved, NZ - 1 - sz, sz), cc, sx + jnp.where(moved, NX, 0))
    barrier = pltpu.get_barrier_semaphore()
    group = [lax.rem(p + i, GROUP) for i in range(GROUP)]
    group_dev = [(sx * GROUP + there, hy) for there in group]
    cross_dev = [at(sx + i, sz, sc, hy) for i in range(NX)]
    head_dev = [at(sx, sz, sc, hy + i) for i in range(NY)]
    greeted = group_dev[1:] + cross_dev[1:] + head_dev[1:] + [swap_to, swap_from]
    for device in greeted:
        pl.semaphore_signal(barrier, inc=1, device_id=device, device_id_type=MESH)

    rows = lax.broadcasted_iota(jnp.int32, (TOK, TOK), 0)
    cols = lax.broadcasted_iota(jnp.int32, (TOK, TOK), 1)
    lower = rows >= cols
    ld = jnp.concatenate([ld_ref[...], jnp.zeros((8 - HEADS, TOK), F32)], axis=0)
    wrow = dot(ld, (rows <= cols).astype(F32), precision=HIGHEST)
    within = dot(lower.astype(F32), ld, NT, precision=HIGHEST)
    for h in range(HEADS):
        dsr[h] = jnp.broadcast_to(wrow[h:h + 1, TOK - 1:TOK], (1, HD))

    loads["k"].wait()
    loads["v"].wait()
    fade = jnp.exp(within[TOK - 1:TOK, :] - within)
    for h in range(HEADS):
        lanes = slice(h * HD, (h + 1) * HD)
        kd = (k[:, lanes].astype(F32) * fade[:, h:h + 1]).astype(BF16)
        st[h * 4:h * 4 + 4] = dot(kd, v[:, lanes], TN).astype(BF16).reshape(4, SLICE, HD)

    pl.semaphore_wait(barrier, len(greeted))

    right_z, left_z = at(sx, sz + 1, sc, hy), at(sx, sz - 1, sc, hy)
    right_x, left_x = at(sx + 1, sz, sc, hy), at(sx - 1, sz, sc, hy)
    right_y, left_y = at(sx, sz, sc, hy + 1), at(sx, sz, sc, hy - 1)

    s_wz = Stream(wbuf.at[0, pl.ds(0, NZ - 1), 0])
    s_wx = Stream(wbuf.at[pl.ds(0, NX - 1), :, 0])
    s_wc = Stream(wbuf.at[:, :, 0])
    s_kz = Stream(kvb.at[pl.ds(0, NZ - 1), :, 0])
    s_kc = Stream(kvb.at[:, :, 0])
    wc_came, kc_came = new_sem(), new_sem()
    wx_came = {1: new_sem(), -1: new_sem()}

    def wz(step, way):
        origin = lax.rem(sz - way * (step - 1) + NZ, NZ)
        if step < NZ // 2:
            part = wbuf.at[sx, origin, sc]
        else:
            part = wbuf.at[sx, origin, sc, pl.ds(0 if way == 1 else 32, 32)]
        return s_wz.send(part, part, right_z if way == 1 else left_z, new_sem())

    def wx_first(origin):
        part = wbuf.at[sx, origin, sc]
        for way in (1, -1):
            s_wx.send(part, part, right_x if way == 1 else left_x, wx_came[way])

    def wx_second(way):
        part = wbuf.at[lax.rem(sx - way + NX, NX), pl.ds(0 if way == 1 else NZ // 2, NZ // 2), sc]
        return s_wx.send(part, part, right_x if way == 1 else left_x, new_sem())

    def kz(step, way, half):
        origin = lax.rem(sz - way * (step - 1) + NZ, NZ)
        part = kvb.at[kslot(origin), pl.ds(half * 2, 2), cc]
        return s_kz.send(part, part, right_z if way == 1 else left_z, new_sem())

    def w_sibling(part):
        s_wc.send(part, part, home, wc_came)

    def k_sibling(part):
        s_kc.send(part, part, home, kc_came)

    s_dec, dec_came = Stream(dec.at[pl.ds(0, GROUP - 1)]), new_sem()
    for i in range(1, GROUP):
        s_dec.send(dsr.at[group[i] // (GROUP // HEADS)], dec.at[p], group_dev[i], dec_came)
    dec[p] = dsr[p // (GROUP // HEADS)]
    s_st, st_came = Stream(rs.at[pl.ds(0, GROUP - 1)]), new_sem()
    for i in range(1, GROUP):
        s_st.send(st.at[group[i]], rs.at[p], group_dev[i], st_came)
    rs[p] = st[p]

    loads["w"].wait()
    c_wz = {(1, way): wz(1, way) for way in (1, -1)}

    def wz_step(step):
        for way in (1, -1):
            c_wz[step, way].wait_recv()
            if step < NZ // 2:
                c_wz[step + 1, way] = wz(step + 1, way)
    loads["q"].wait()
    for h in range(HEADS):
        lanes = slice(h * HD, (h + 1) * HD)
        spread = within[:, h:h + 1] - wrow[h:h + 1, :]
        factor = jnp.exp(jnp.where(lower, spread, -1e30))
        scores = dot(q[:, lanes], k[:, lanes], NT)
        intra[:, lanes] = dot((scores * factor).astype(BF16), v[:, lanes])

    loads["kw"].wait()
    c_swap = Stream(kin).send(kin, kvb.at[4 * (hy // 4) + lax.rem(sz, 4), swap_x, sc], swap_to, new_sem())
    loads["g"].wait()
    opened = g[...].astype(F32)
    acc[...] = opened / (1.0 + jnp.exp(-opened))

    arrived(dec.at[pl.ds(0, GROUP - 1)], dec_came)
    arrived(rs.at[pl.ds(0, GROUP - 1)], st_came)
    state = jnp.zeros((SLICE, HD), F32)
    passed = jnp.zeros((1, HD), F32)
    before = []
    for i in range(GROUP):
        ex[i] = state
        before.append(passed)
        step = dec[i]
        state = jnp.exp(step) * state + rs[i].astype(F32)
        passed = passed + step
    xs[sx, 0:SLICE, :] = state
    xs[sx, SLICE:SLICE + 8, :] = jnp.broadcast_to(passed, (8, HD))
    s_xs, xs_came = Stream(xs.at[pl.ds(0, NX - 1)]), new_sem()
    for i in range(1, NX):
        s_xs.send(xs.at[sx], xs.at[sx], cross_dev[i], xs_came)

    wz_step(1)

    arrived(xs.at[pl.ds(0, NX - 1)], xs_came)
    base = jnp.zeros((SLICE, HD), F32)
    for x in range(NX - 1):
        fresh = jnp.exp(xs[x, SLICE:SLICE + 1, :]) * base + xs[x, 0:SLICE, :]
        base = jnp.where(x < sx, fresh, base)
    for i in range(GROUP):
        ob[i] = (ex[i] + jnp.exp(before[i]) * base).astype(BF16)
    s_inc, inc_came = Stream(ob.at[pl.ds(0, GROUP - 1)]), new_sem()
    for i in range(1, GROUP):
        s_inc.send(ob.at[group[i]], inc.at[p], group_dev[i], inc_came)
    inc[p] = ob[p]

    c_swap.wait_recv()
    own_kv = kvb.at[kslot(sz), sx, cc]
    s_kx, kx_came = Stream(kvb.at[0, pl.ds(0, NX - 1), 0]), new_sem()
    for i in range(1, NX):
        s_kx.send(own_kv, own_kv, cross_dev[i], kx_came)
    for step in (0, -1, 1):
        wx_first(lax.rem(sz + step + NZ, NZ))
    wz_step(2)
    for step in (-2, 2):
        wx_first(lax.rem(sz + step + NZ, NZ))
    wz_step(3)
    for step in (-3, 3):
        wx_first(lax.rem(sz + step + NZ, NZ))
    loads["r"].wait()
    arrived(kvb.at[0, pl.ds(0, NX - 1), 0], kx_came)
    arrived(inc.at[pl.ds(0, GROUP - 1)], inc_came)

    c_kz = {}
    c_wx = {}

    def kz_step(step, half):
        for way in (1, -1):
            if (step, way, half) not in c_kz:
                continue
            c_kz[step, way, half].wait_recv()
            if step + 1 < NZ // 2 or (step + 1 == NZ // 2 and half == (0 if way == 1 else 1)):
                c_kz[step + 1, way, half] = kz(step + 1, way, half)
            origin = lax.rem(sz - way * step + NZ, NZ)
            k_sibling(kvb.at[kslot(origin), pl.ds(half * 2, 2), cc])

    def wx_step(step):
        for way in (1, -1):
            origin = lax.rem(sx - way * step + NX, NX)
            if step == 1:
                arrived(wbuf.at[0, :, 0], wx_came[way])
                c_wx[way] = wx_second(way)
                w_sibling(wbuf.at[origin, :, sc])
            else:
                c_wx[way].wait_recv()
                half = pl.ds(0 if way == 1 else NZ // 2, NZ // 2)
                w_sibling(wbuf.at[origin, half, sc])

    s_mix, c_mix = Stream(abuf.at[pl.ds(0, NY - 1)]), {}

    def far(chunk):
        return 1 if chunk < CHUNKS // 2 else -1

    def mix_send(step, way, chunk):
        if step == NY // 2 and way != far(chunk):
            return
        origin = lax.rem(hy - way * (step - 1) + NY, NY)
        part = abuf.at[origin, pl.ds(chunk * ROWS, ROWS)]
        c_mix[step, way, chunk] = s_mix.send(part, part, right_y if way == 1 else left_y, new_sem())

    grown = jnp.exp(within)
    for chunk in ORDER:
        span = slice(chunk * ROWS, (chunk + 1) * ROWS)
        for h in range(HEADS):
            lanes = slice(h * HD, (h + 1) * HD)
            entering = inc[4 * h:4 * h + 4].reshape(HD, HD)
            kept = intra[span, lanes] + grown[span, h:h + 1] * dot(q[span, lanes], entering)
            scale = lax.rsqrt(jnp.mean(kept * kept, axis=1, keepdims=True) + 1e-6)
            abuf[hy, span, lanes] = (acc[span, lanes] * (kept * scale)).astype(BF16)
        for way in (1, -1):
            mix_send(1, way, chunk)
        if chunk < 2:
            for way in (1, -1):
                c_kz[1, way, chunk] = kz(1, way, chunk)

    wz_step(4)
    wx_first(lax.rem(sz + NZ // 2, NZ))
    w_sibling(wbuf.at[sx, :, sc])
    k_sibling(kvb.at[kslot(sz), :, cc])
    service = {
        0: (lambda: kz_step(1, 0),), 1: (lambda: kz_step(1, 1),),
        3: (lambda: kz_step(2, 0), lambda: wx_step(1)), 4: (lambda: kz_step(2, 1),),
        6: (lambda: kz_step(3, 0),), 7: (lambda: kz_step(3, 1),),
        9: (lambda: kz_step(4, 0), lambda: kz_step(4, 1), lambda: wx_step(2)),
    }
    for step in range(1, NY // 2):
        for n, chunk in enumerate(ORDER):
            for way in (1, -1):
                c_mix[step, way, chunk].wait_recv()
                mix_send(step + 1, way, chunk)
            for job in service.get((step - 1) * CHUNKS + n, ()):
                job()

    arrived(wbuf.at[:, :, 0], wc_came)

    def weight(origin):
        return wbuf[origin // 2, pl.ds(lax.rem(origin, 2) * 4, 4)].reshape(WID, WID)

    acc[...] = res[...].astype(F32)

    def projected(i, carry):
        origin = lax.rem(hy - (NY // 2 - 1) + i + NY, NY)
        acc[...] += dot(abuf[origin], weight(origin))
        return carry

    lax.fori_loop(0, NY - 1, projected, 0)
    arrived(kvb.at[:, :, 0], kc_came)

    last = lax.rem(hy + NY // 2, NY)
    s_red, c_red = Stream(red_out.at[pl.ds(0, NY - 1)]), {}

    def cache_weight(origin):
        return kvb[pl.ds(4 * (origin // 4), 4), lax.rem(origin, NX)].reshape(WID, 2 * HD)

    def reduce_send(step, way, chunk):
        span = slice(chunk * ROWS, (chunk + 1) * ROWS)
        slot = step * 2 + (0 if way == 1 else 1)
        origin = lax.rem(hy + way * (NY // 2 - step) + NY, NY)
        value = dot(hg[span, :], cache_weight(origin))
        if (step - 1, way, chunk) in c_red:
            c_red[step - 1, way, chunk].wait_recv()
            value = value + red_in[slot - 2, span, :].astype(F32)
        red_out[slot, span, :] = value.astype(BF16)
        c_red[step, way, chunk] = s_red.send(
            red_out.at[slot, pl.ds(chunk * ROWS, ROWS)], red_in.at[slot, pl.ds(chunk * ROWS, ROWS)],
            right_y if way == 1 else left_y, new_sem(),
        )

    gain = gain_ref[...].astype(F32).reshape(1, WID)
    for chunk in ORDER:
        span = slice(chunk * ROWS, (chunk + 1) * ROWS)
        c_mix[NY // 2, far(chunk), chunk].wait_recv()
        hidden = (acc[span, :] + dot(abuf[last, span, :], weight(last))).astype(BF16).astype(F32)
        hg[span, :] = (hidden * gain).astype(BF16)
        scol[span, :] = jnp.broadcast_to(jnp.sum(hidden * hidden, axis=1, keepdims=True), (ROWS, HD))
        reduce_send(0, far(chunk), chunk)
        reduce_send(1, -far(chunk), chunk)
    sq[hy] = jnp.transpose(scol[...])[0:8, :]
    s_sq, sq_came = Stream(sq.at[pl.ds(0, NY - 1)]), new_sem()
    for i in range(1, NY):
        s_sq.send(sq.at[hy], sq.at[hy], head_dev[i], sq_came)
    for chunk in ORDER:
        reduce_send(1, far(chunk), chunk)
    for step in range(2, NY // 2):
        for late in (False, True):
            for chunk in ORDER:
                reduce_send(step, far(chunk) if late else -far(chunk), chunk)
    arrived(sq.at[pl.ds(0, NY - 1)], sq_came)
    total = sq[0]
    for y in range(1, NY):
        total = total + sq[y]
    inverse = jnp.transpose(lax.rsqrt(total / (WID * NY) + 1e-6))
    for chunk in ORDER:
        span = slice(chunk * ROWS, (chunk + 1) * ROWS)
        value = dot(hg[span, :], cache_weight(hy))
        for way in (1, -1):
            c_red[NY // 2 - 1, way, chunk].wait_recv()
            slot = NY - 2 + (0 if way == 1 else 1)
            value = value + red_in[slot, span, :].astype(F32)
        out_ref[span, :] = (value * inverse[span, 0:1]).astype(BF16)

    assert count[0] <= COPIES, count[0]
    for whole, sent in drains:
        pltpu.make_async_remote_copy(
            src_ref=whole, dst_ref=whole, send_sem=sent, recv_sem=sent,
            device_id=home, device_id_type=MESH,
        ).wait_send()


def on_device(queries, keys, values, gate, residual, log_decay, out_weight, norm_gain, kv_weight):
    hbm = pl.BlockSpec(memory_space=pltpu.HBM)
    vmem = pl.BlockSpec(memory_space=pltpu.VMEM)
    block = pltpu.VMEM((TOK, WID), BF16)
    reds = pltpu.VMEM((NY, TOK, 2 * HD), BF16)
    slices = pltpu.VMEM((GROUP, SLICE, HD), BF16)
    both = pl.pallas_call(
        layer_kernel,
        out_shape=jax.ShapeDtypeStruct((TOK, 2 * HD), BF16),
        in_specs=[hbm] * 5 + [vmem, hbm, vmem, hbm],
        out_specs=vmem,
        scratch_shapes=[
            block, block, block, block, block,
            pltpu.VMEM((NX, NZ, NC, 64, WID), BF16),
            pltpu.VMEM((NZ, NX, NC, 64, 2 * HD), BF16),
            pltpu.VMEM((64, 2 * HD), BF16),
            slices,
            slices,
            pltpu.VMEM((HEADS, 1, HD), F32),
            pltpu.VMEM((GROUP, 1, HD), F32),
            pltpu.VMEM((NX, SLICE + 8, HD), F32),
            pltpu.VMEM((GROUP, SLICE, HD), F32),
            slices,
            slices,
            pltpu.VMEM((TOK, WID), F32),
            pltpu.VMEM((NY, TOK, WID), BF16),
            pltpu.VMEM((TOK, WID), F32),
            block,
            reds, reds,
            pltpu.VMEM((TOK, HD), F32),
            pltpu.VMEM((NY, 8, TOK), F32),
            pltpu.SemaphoreType.DMA((7,)),
            pltpu.SemaphoreType.DMA((COPIES,)),
        ],
        compiler_params=pltpu.CompilerParams(
            collective_id=0, has_side_effects=True, vmem_limit_bytes=62 << 20
        ),
    )(
        queries, keys, values, gate, residual, log_decay.T, out_weight, norm_gain, kv_weight,
    )
    return both[:, :HD], both[:, HD:]


def solution(mesh):
    placed = (P("seq", "head"),) * 7 + (P("head"), P("seq", "head"))
    return jax.shard_map(
        on_device,
        mesh=mesh,
        in_specs=placed,
        out_specs=(P("seq", "head"), P("seq", "head")),
        check_vma=False,
    )
```

```python
import functools

import jax
import jax.numpy as jnp
from jax import lax
from jax.experimental import pallas as pl
from jax.experimental.pallas import tpu as pltpu
from jax.sharding import PartitionSpec as P

MESH = pl.DeviceIdType.MESH
HIGHEST = lax.Precision.HIGHEST
F32, BF16 = jnp.float32, jnp.bfloat16

NX, NZ, NC, NY = 4, 8, 2, 8
GROUP = NZ * NC
TOK, WID, HEADS, HD = 256, 512, 4, 128
SLICE = HEADS * HD // GROUP
CHUNKS = 4
ROWS = TOK // CHUNKS
COPIES = 105
ORDER = (0, 2, 1, 3)


def dot(a, b, dims=(((1,), (0,)), ((), ())), precision=None):
    return lax.dot_general(a, b, dims, precision=precision, preferred_element_type=F32)


def farthest(size):
    return sorted(range(1, size), key=lambda i: (-min(i, size - i), i))


NT = (((1,), (1,)), ((), ()))
TN = (((0,), (0,)), ((), ()))


def layer_kernel(
    q_h, k_h, v_h, g_h, r_h, ld_ref, ow_h, gain_ref, kw_h,
    out_ref,
    q, k, v, g, res, wbuf, kvb, kin, st, rs, dsr, dec, xs, ex, ob, inc,
    intra, abuf, acc, hg, red_out, red_in, part, scol, sq,
    lsem, sem,
):
    seq, hy = lax.axis_index("seq"), lax.axis_index("head")
    sx, p = seq // GROUP, lax.rem(seq, GROUP)
    sz, sc = p // NC, lax.rem(p, NC)
    cc = 1 - sc

    def at(x, z, c, y):
        return (lax.rem(x + NX, NX) * GROUP + lax.rem(z + NZ, NZ) * NC + c, lax.rem(y + NY, NY))

    count = [0]

    def new_sem():
        count[0] += 1
        return sem.at[count[0] - 1]

    home = at(sx, sz, cc, hy)
    drains = []

    class Stream:
        def __init__(self, whole):
            self.sent = new_sem()
            drains.append((whole, self.sent))

        def send(self, src, dst, device, came):
            copy = pltpu.make_async_remote_copy(
                src_ref=src, dst_ref=dst, send_sem=self.sent, recv_sem=came,
                device_id=device, device_id_type=MESH,
            )
            copy.start()
            return copy

    def arrived(whole, came):
        pltpu.make_async_remote_copy(
            src_ref=whole, dst_ref=whole, send_sem=came, recv_sem=came,
            device_id=home, device_id_type=MESH,
        ).wait_recv()

    loads = {}
    for i, (name, src, dst) in enumerate((
        ("w", ow_h, wbuf.at[sx, sz, sc]), ("kw", kw_h, kin), ("k", k_h, k), ("v", v_h, v),
        ("q", q_h, q), ("g", g_h, g), ("r", r_h, res),
    )):
        loads[name] = pltpu.make_async_copy(src, dst, lsem.at[i])
        loads[name].start()

    swap_x, swap_z = lax.rem(hy, NX), jnp.where(hy < NX, sz, NZ - 1 - sz)
    swap_to = at(swap_x, swap_z, cc, 2 * sx + sz // 4)

    def kslot(z):
        return jnp.where((z // 4) != lax.rem(hy, 2), NZ - 1 - lax.rem(z, 4), lax.rem(z, 4))

    moved = (sz // 4) != lax.rem(hy, 2)
    swap_from = at(hy // 2, jnp.where(moved, NZ - 1 - sz, sz), cc, sx + jnp.where(moved, NX, 0))
    barrier = pltpu.get_barrier_semaphore()
    group = [lax.rem(p + i, GROUP) for i in range(GROUP)]
    group_dev = [(sx * GROUP + there, hy) for there in group]
    cross_dev = [at(sx + i, sz, sc, hy) for i in range(NX)]
    head_dev = [at(sx, sz, sc, hy + i) for i in range(NY)]
    greeted = group_dev[1:] + cross_dev[1:] + head_dev[1:] + [swap_to, swap_from]
    for device in greeted:
        pl.semaphore_signal(barrier, inc=1, device_id=device, device_id_type=MESH)

    rows = lax.broadcasted_iota(jnp.int32, (TOK, TOK), 0)
    cols = lax.broadcasted_iota(jnp.int32, (TOK, TOK), 1)
    lower = rows >= cols
    ld = jnp.concatenate([ld_ref[...], jnp.zeros((8 - HEADS, TOK), F32)], axis=0)
    wrow = dot(ld, (rows <= cols).astype(F32), precision=HIGHEST)
    within = dot(lower.astype(F32), ld, NT, precision=HIGHEST)
    for h in range(HEADS):
        dsr[h] = jnp.broadcast_to(wrow[h:h + 1, TOK - 1:TOK], (1, HD))

    loads["k"].wait()
    loads["v"].wait()
    fade = jnp.exp(within[TOK - 1:TOK, :] - within)
    for h in range(HEADS):
        lanes = slice(h * HD, (h + 1) * HD)
        kd = (k[:, lanes].astype(F32) * fade[:, h:h + 1]).astype(BF16)
        st[h * 4:h * 4 + 4] = dot(kd, v[:, lanes], TN).astype(BF16).reshape(4, SLICE, HD)

    pl.semaphore_wait(barrier, len(greeted))

    right_z, left_z = at(sx, sz + 1, sc, hy), at(sx, sz - 1, sc, hy)
    right_x, left_x = at(sx + 1, sz, sc, hy), at(sx - 1, sz, sc, hy)
    right_y, left_y = at(sx, sz, sc, hy + 1), at(sx, sz, sc, hy - 1)

    s_wz = Stream(wbuf.at[0, pl.ds(0, NZ - 1), 0])
    s_wx = Stream(wbuf.at[pl.ds(0, NX - 1), :, 0])
    s_wc = Stream(wbuf.at[:, :, 0])
    s_kz = Stream(kvb.at[pl.ds(0, NZ - 1), :, 0])
    s_kc = Stream(kvb.at[:, :, 0])
    wc_came, kc_came = new_sem(), new_sem()
    wx_came = {1: new_sem(), -1: new_sem()}

    def wz(step, way):
        origin = lax.rem(sz - way * (step - 1) + NZ, NZ)
        if step < NZ // 2:
            part = wbuf.at[sx, origin, sc]
        else:
            part = wbuf.at[sx, origin, sc, pl.ds(0 if way == 1 else 32, 32)]
        return s_wz.send(part, part, right_z if way == 1 else left_z, new_sem())

    def wx_first(origin):
        part = wbuf.at[sx, origin, sc]
        for way in (1, -1):
            s_wx.send(part, part, right_x if way == 1 else left_x, wx_came[way])

    def wx_second(way):
        part = wbuf.at[lax.rem(sx - way + NX, NX), pl.ds(0 if way == 1 else NZ // 2, NZ // 2), sc]
        return s_wx.send(part, part, right_x if way == 1 else left_x, new_sem())

    def kz(step, way, half):
        origin = lax.rem(sz - way * (step - 1) + NZ, NZ)
        part = kvb.at[kslot(origin), pl.ds(half * 2, 2), cc]
        return s_kz.send(part, part, right_z if way == 1 else left_z, new_sem())

    def w_sibling(part):
        s_wc.send(part, part, home, wc_came)

    def k_sibling(part):
        s_kc.send(part, part, home, kc_came)

    s_dec, dec_came = Stream(dec.at[pl.ds(0, GROUP - 1)]), new_sem()
    for i in farthest(GROUP):
        s_dec.send(dsr.at[group[i] // (GROUP // HEADS)], dec.at[p], group_dev[i], dec_came)
    dec[p] = dsr[p // (GROUP // HEADS)]
    s_st, st_came = Stream(rs.at[pl.ds(0, GROUP - 1)]), new_sem()
    for i in farthest(GROUP):
        s_st.send(st.at[group[i]], rs.at[p], group_dev[i], st_came)
    rs[p] = st[p]

    loads["w"].wait()
    c_wz = {(1, way): wz(1, way) for way in (1, -1)}

    def wz_step(step):
        for way in (1, -1):
            c_wz[step, way].wait_recv()
            if step < NZ // 2:
                c_wz[step + 1, way] = wz(step + 1, way)
    loads["q"].wait()
    for h in range(HEADS):
        lanes = slice(h * HD, (h + 1) * HD)
        spread = within[:, h:h + 1] - wrow[h:h + 1, :]
        factor = jnp.exp(jnp.where(lower, spread, -1e30))
        scores = dot(q[:, lanes], k[:, lanes], NT)
        intra[:, lanes] = dot((scores * factor).astype(BF16), v[:, lanes])

    loads["kw"].wait()
    c_swap = Stream(kin).send(kin, kvb.at[4 * (hy // 4) + lax.rem(sz, 4), swap_x, sc], swap_to, new_sem())
    loads["g"].wait()
    opened = g[...].astype(F32)
    acc[...] = opened / (1.0 + jnp.exp(-opened))

    arrived(dec.at[pl.ds(0, GROUP - 1)], dec_came)
    arrived(rs.at[pl.ds(0, GROUP - 1)], st_came)
    state = jnp.zeros((SLICE, HD), F32)
    passed = jnp.zeros((1, HD), F32)
    before = []
    for i in range(GROUP):
        ex[i] = state
        before.append(passed)
        step = dec[i]
        state = jnp.exp(step) * state + rs[i].astype(F32)
        passed = passed + step
    xs[sx, 0:SLICE, :] = state
    xs[sx, SLICE:SLICE + 8, :] = jnp.broadcast_to(passed, (8, HD))
    s_xs, xs_came = Stream(xs.at[pl.ds(0, NX - 1)]), new_sem()
    for i in farthest(NX):
        s_xs.send(xs.at[sx], xs.at[sx], cross_dev[i], xs_came)

    wz_step(1)

    arrived(xs.at[pl.ds(0, NX - 1)], xs_came)
    base = jnp.zeros((SLICE, HD), F32)
    for x in range(NX - 1):
        fresh = jnp.exp(xs[x, SLICE:SLICE + 1, :]) * base + xs[x, 0:SLICE, :]
        base = jnp.where(x < sx, fresh, base)
    for i in range(GROUP):
        ob[i] = (ex[i] + jnp.exp(before[i]) * base).astype(BF16)
    s_inc, inc_came = Stream(ob.at[pl.ds(0, GROUP - 1)]), new_sem()
    for i in farthest(GROUP):
        s_inc.send(ob.at[group[i]], inc.at[p], group_dev[i], inc_came)
    inc[p] = ob[p]

    c_swap.wait_recv()
    own_kv = kvb.at[kslot(sz), sx, cc]
    s_kx, kx_came = Stream(kvb.at[0, pl.ds(0, NX - 1), 0]), new_sem()
    for i in farthest(NX):
        s_kx.send(own_kv, own_kv, cross_dev[i], kx_came)
    for step in (0, -1, 1):
        wx_first(lax.rem(sz + step + NZ, NZ))
    wz_step(2)
    for step in (-2, 2):
        wx_first(lax.rem(sz + step + NZ, NZ))
    wz_step(3)
    for step in (-3, 3):
        wx_first(lax.rem(sz + step + NZ, NZ))
    loads["r"].wait()
    arrived(kvb.at[0, pl.ds(0, NX - 1), 0], kx_came)
    arrived(inc.at[pl.ds(0, GROUP - 1)], inc_came)

    c_kz = {}
    c_wx = {}

    def kz_step(step, half):
        for way in (1, -1):
            if (step, way, half) not in c_kz:
                continue
            c_kz[step, way, half].wait_recv()
            if step + 1 < NZ // 2 or (step + 1 == NZ // 2 and half == (0 if way == 1 else 1)):
                c_kz[step + 1, way, half] = kz(step + 1, way, half)
            origin = lax.rem(sz - way * step + NZ, NZ)
            k_sibling(kvb.at[kslot(origin), pl.ds(half * 2, 2), cc])

    def wx_step(step):
        for way in (1, -1):
            origin = lax.rem(sx - way * step + NX, NX)
            if step == 1:
                arrived(wbuf.at[0, :, 0], wx_came[way])
                c_wx[way] = wx_second(way)
                w_sibling(wbuf.at[origin, :, sc])
            else:
                c_wx[way].wait_recv()
                half = pl.ds(0 if way == 1 else NZ // 2, NZ // 2)
                w_sibling(wbuf.at[origin, half, sc])

    s_mix, c_mix = Stream(abuf.at[pl.ds(0, NY - 1)]), {}

    def far(chunk):
        return 1 if chunk < CHUNKS // 2 else -1

    def mix_send(step, way, chunk):
        if step == NY // 2 and way != far(chunk):
            return
        origin = lax.rem(hy - way * (step - 1) + NY, NY)
        part = abuf.at[origin, pl.ds(chunk * ROWS, ROWS)]
        c_mix[step, way, chunk] = s_mix.send(part, part, right_y if way == 1 else left_y, new_sem())

    grown = jnp.exp(within)
    for chunk in ORDER:
        span = slice(chunk * ROWS, (chunk + 1) * ROWS)
        for h in range(HEADS):
            lanes = slice(h * HD, (h + 1) * HD)
            entering = inc[4 * h:4 * h + 4].reshape(HD, HD)
            kept = intra[span, lanes] + grown[span, h:h + 1] * dot(q[span, lanes], entering)
            scale = lax.rsqrt(jnp.mean(kept * kept, axis=1, keepdims=True) + 1e-6)
            abuf[hy, span, lanes] = (acc[span, lanes] * (kept * scale)).astype(BF16)
        for way in (1, -1):
            mix_send(1, way, chunk)
        if chunk < 2:
            for way in (1, -1):
                c_kz[1, way, chunk] = kz(1, way, chunk)

    wz_step(4)
    wx_first(lax.rem(sz + NZ // 2, NZ))
    w_sibling(wbuf.at[sx, :, sc])
    k_sibling(kvb.at[kslot(sz), :, cc])
    service = {
        0: (lambda: kz_step(1, 0),), 1: (lambda: kz_step(1, 1),),
        3: (lambda: kz_step(2, 0), lambda: wx_step(1)), 4: (lambda: kz_step(2, 1),),
        6: (lambda: kz_step(3, 0),), 7: (lambda: kz_step(3, 1),),
        9: (lambda: kz_step(4, 0), lambda: kz_step(4, 1), lambda: wx_step(2)),
    }
    for step in range(1, NY // 2):
        for n, chunk in enumerate(ORDER):
            for way in (1, -1):
                c_mix[step, way, chunk].wait_recv()
                mix_send(step + 1, way, chunk)
            for job in service.get((step - 1) * CHUNKS + n, ()):
                job()

    arrived(wbuf.at[:, :, 0], wc_came)

    def weight(origin):
        return wbuf[origin // 2, pl.ds(lax.rem(origin, 2) * 4, 4)].reshape(WID, WID)

    acc[...] = res[...].astype(F32)

    def projected(i, carry):
        origin = lax.rem(hy - (NY // 2 - 1) + i + NY, NY)
        acc[...] += dot(abuf[origin], weight(origin))
        return carry

    lax.fori_loop(0, NY - 1, projected, 0)
    arrived(kvb.at[:, :, 0], kc_came)

    last = lax.rem(hy + NY // 2, NY)
    s_red, c_red = Stream(red_out.at[pl.ds(0, NY - 1)]), {}

    def cache_weight(origin):
        return kvb[pl.ds(4 * (origin // 4), 4), lax.rem(origin, NX)].reshape(WID, 2 * HD)

    def toward(step, way):
        return lax.rem(hy + way * (NY // 2 - step) + NY, NY)

    def partial(origin, span):
        return dot(hg[span, :], cache_weight(origin))

    def side(way):
        return 0 if way == 1 else 1

    def rows_of(chunk):
        return slice(chunk * ROWS, (chunk + 1) * ROWS)

    def reduce_send(step, way, chunk, value):
        slot = step * 2 + side(way)
        if (step - 1, way, chunk) in c_red:
            c_red[step - 1, way, chunk].wait_recv()
            value = value + red_in[slot - 2, rows_of(chunk), :].astype(F32)
        red_out[slot, rows_of(chunk), :] = value.astype(BF16)
        c_red[step, way, chunk] = s_red.send(
            red_out.at[slot, pl.ds(chunk * ROWS, ROWS)], red_in.at[slot, pl.ds(chunk * ROWS, ROWS)],
            right_y if way == 1 else left_y, new_sem(),
        )

    gain = gain_ref[...].astype(F32).reshape(1, WID)
    for chunk in ORDER:
        span = rows_of(chunk)
        c_mix[NY // 2, far(chunk), chunk].wait_recv()
        hidden = (acc[span, :] + dot(abuf[last, span, :], weight(last))).astype(BF16).astype(F32)
        hg[span, :] = (hidden * gain).astype(BF16)
        scol[span, :] = jnp.broadcast_to(jnp.sum(hidden * hidden, axis=1, keepdims=True), (ROWS, HD))
        for step, way in ((0, far(chunk)), (1, -far(chunk))):
            reduce_send(step, way, chunk, partial(toward(step, way), span))
    for way in (1, -1):
        half = slice(0, TOK // 2) if way == 1 else slice(TOK // 2, TOK)
        part[side(way), half, :] = partial(toward(1, way), half)
    for chunk in ORDER:
        way = far(chunk)
        reduce_send(1, way, chunk, part[side(way), rows_of(chunk), :])
    sq[hy] = jnp.transpose(scol[...])[0:8, :]
    s_sq, sq_came = Stream(sq.at[pl.ds(0, NY - 1)]), new_sem()
    for i in farthest(NY):
        s_sq.send(sq.at[hy], sq.at[hy], head_dev[i], sq_came)
    for step in range(2, NY // 2):
        for way in (1, -1):
            part[side(way)] = partial(toward(step, way), slice(None))
        for late in (False, True):
            for chunk in ORDER:
                way = far(chunk) if late else -far(chunk)
                reduce_send(step, way, chunk, part[side(way), rows_of(chunk), :])
    part[0] = partial(hy, slice(None))
    arrived(sq.at[pl.ds(0, NY - 1)], sq_came)
    total = sq[0]
    for y in range(1, NY):
        total = total + sq[y]
    inverse = jnp.transpose(lax.rsqrt(total / (WID * NY) + 1e-6))
    for chunk in ORDER:
        span = rows_of(chunk)
        value = part[0, span, :]
        for way in (1, -1):
            c_red[NY // 2 - 1, way, chunk].wait_recv()
            value = value + red_in[NY - 2 + side(way), span, :].astype(F32)
        out_ref[span, :] = (value * inverse[span, 0:1]).astype(BF16)

    assert count[0] <= COPIES, count[0]
    for whole, sent in drains:
        pltpu.make_async_remote_copy(
            src_ref=whole, dst_ref=whole, send_sem=sent, recv_sem=sent,
            device_id=home, device_id_type=MESH,
        ).wait_send()


def on_device(queries, keys, values, gate, residual, log_decay, out_weight, norm_gain, kv_weight):
    hbm = pl.BlockSpec(memory_space=pltpu.HBM)
    vmem = pl.BlockSpec(memory_space=pltpu.VMEM)
    block = pltpu.VMEM((TOK, WID), BF16)
    reds = pltpu.VMEM((NY, TOK, 2 * HD), BF16)
    slices = pltpu.VMEM((GROUP, SLICE, HD), BF16)
    both = pl.pallas_call(
        layer_kernel,
        out_shape=jax.ShapeDtypeStruct((TOK, 2 * HD), BF16),
        in_specs=[hbm] * 5 + [vmem, hbm, vmem, hbm],
        out_specs=vmem,
        scratch_shapes=[
            block, block, block, block, block,
            pltpu.VMEM((NX, NZ, NC, 64, WID), BF16),
            pltpu.VMEM((NZ, NX, NC, 64, 2 * HD), BF16),
            pltpu.VMEM((64, 2 * HD), BF16),
            slices,
            slices,
            pltpu.VMEM((HEADS, 1, HD), F32),
            pltpu.VMEM((GROUP, 1, HD), F32),
            pltpu.VMEM((NX, SLICE + 8, HD), F32),
            pltpu.VMEM((GROUP, SLICE, HD), F32),
            slices,
            slices,
            pltpu.VMEM((TOK, WID), F32),
            pltpu.VMEM((NY, TOK, WID), BF16),
            pltpu.VMEM((TOK, WID), F32),
            block,
            reds, reds,
            pltpu.VMEM((2, TOK, 2 * HD), F32),
            pltpu.VMEM((TOK, HD), F32),
            pltpu.VMEM((NY, 8, TOK), F32),
            pltpu.SemaphoreType.DMA((7,)),
            pltpu.SemaphoreType.DMA((COPIES,)),
        ],
        compiler_params=pltpu.CompilerParams(
            collective_id=0, has_side_effects=True, vmem_limit_bytes=62 << 20
        ),
    )(
        queries, keys, values, gate, residual, log_decay.T, out_weight, norm_gain, kv_weight,
    )
    return both[:, :HD], both[:, HD:]


def solution(mesh):
    placed = (P("seq", "head"),) * 7 + (P("head"), P("seq", "head"))
    return jax.shard_map(
        on_device,
        mesh=mesh,
        in_specs=placed,
        out_specs=(P("seq", "head"), P("seq", "head")),
        check_vma=False,
    )
```

```python
import functools

import jax
import jax.numpy as jnp
from jax import lax
from jax.experimental import pallas as pl
from jax.experimental.pallas import tpu as pltpu
from jax.sharding import PartitionSpec as P

MESH = pl.DeviceIdType.MESH
HIGHEST = lax.Precision.HIGHEST
F32, BF16 = jnp.float32, jnp.bfloat16

NX, NZ, NC, NY = 4, 8, 2, 8
GROUP = NZ * NC
TOK, WID, HEADS, HD = 256, 512, 4, 128
SLICE = HEADS * HD // GROUP
CHUNKS = 4
ROWS = TOK // CHUNKS
COPIES = 105
ORDER = (0, 2, 1, 3)


def dot(a, b, dims=(((1,), (0,)), ((), ())), precision=None):
    return lax.dot_general(a, b, dims, precision=precision, preferred_element_type=F32)


def farthest(size):
    return sorted(range(1, size), key=lambda i: (-min(i, size - i), i))


NT = (((1,), (1,)), ((), ()))
TN = (((0,), (0,)), ((), ()))


def layer_kernel(
    q_h, k_h, v_h, g_h, r_h, ld_ref, ow_h, gain_ref, kw_h,
    out_ref,
    q, k, v, g, res, wbuf, kvb, kin, st, rs, dsr, dec, xs, ex, ob, inc,
    intra, abuf, acc, hg, red_out, red_in, part, scol, sq,
    lsem, sem,
):
    seq, hy = lax.axis_index("seq"), lax.axis_index("head")
    sx, p = seq // GROUP, lax.rem(seq, GROUP)
    sz, sc = p // NC, lax.rem(p, NC)
    cc = 1 - sc

    def at(x, z, c, y):
        return (lax.rem(x + NX, NX) * GROUP + lax.rem(z + NZ, NZ) * NC + c, lax.rem(y + NY, NY))

    count = [0]

    def new_sem():
        count[0] += 1
        return sem.at[count[0] - 1]

    home = at(sx, sz, cc, hy)
    drains = []

    class Stream:
        def __init__(self, whole):
            self.sent = new_sem()
            drains.append((whole, self.sent))

        def send(self, src, dst, device, came):
            copy = pltpu.make_async_remote_copy(
                src_ref=src, dst_ref=dst, send_sem=self.sent, recv_sem=came,
                device_id=device, device_id_type=MESH,
            )
            copy.start()
            return copy

    def arrived(whole, came):
        pltpu.make_async_remote_copy(
            src_ref=whole, dst_ref=whole, send_sem=came, recv_sem=came,
            device_id=home, device_id_type=MESH,
        ).wait_recv()

    swap_x, swap_z = lax.rem(hy, NX), jnp.where(hy < NX, sz, NZ - 1 - sz)
    swap_to = at(swap_x, swap_z, cc, 2 * sx + sz // 4)

    def kslot(z):
        return jnp.where((z // 4) != lax.rem(hy, 2), NZ - 1 - lax.rem(z, 4), lax.rem(z, 4))

    moved = (sz // 4) != lax.rem(hy, 2)
    swap_from = at(hy // 2, jnp.where(moved, NZ - 1 - sz, sz), cc, sx + jnp.where(moved, NX, 0))
    barrier = pltpu.get_barrier_semaphore()
    group = [lax.rem(p + i, GROUP) for i in range(GROUP)]
    group_dev = [(sx * GROUP + there, hy) for there in group]
    cross_dev = [at(sx + i, sz, sc, hy) for i in range(NX)]
    head_dev = [at(sx, sz, sc, hy + i) for i in range(NY)]
    greeted = group_dev[1:] + cross_dev[1:] + head_dev[1:] + [swap_to, swap_from]
    for device in greeted:
        pl.semaphore_signal(barrier, inc=1, device_id=device, device_id_type=MESH)

    loads = {}
    for i, (name, src, dst) in enumerate((
        ("w", ow_h, wbuf.at[sx, sz, sc]), ("kw", kw_h, kin), ("k", k_h, k), ("v", v_h, v),
        ("q", q_h, q), ("g", g_h, g), ("r", r_h, res),
    )):
        loads[name] = pltpu.make_async_copy(src, dst, lsem.at[i])
        loads[name].start()

    rows = lax.broadcasted_iota(jnp.int32, (TOK, TOK), 0)
    cols = lax.broadcasted_iota(jnp.int32, (TOK, TOK), 1)
    lower = rows >= cols
    ld = jnp.concatenate([ld_ref[...], jnp.zeros((8 - HEADS, TOK), F32)], axis=0)
    wrow = dot(ld, (rows <= cols).astype(F32), precision=HIGHEST)
    within = dot(lower.astype(F32), ld, NT, precision=HIGHEST)
    for h in range(HEADS):
        dsr[h] = jnp.broadcast_to(wrow[h:h + 1, TOK - 1:TOK], (1, HD))

    loads["k"].wait()
    loads["v"].wait()
    fade = jnp.exp(within[TOK - 1:TOK, :] - within)
    for h in range(HEADS):
        lanes = slice(h * HD, (h + 1) * HD)
        kd = (k[:, lanes].astype(F32) * fade[:, h:h + 1]).astype(BF16)
        st[h * 4:h * 4 + 4] = dot(kd, v[:, lanes], TN).astype(BF16).reshape(4, SLICE, HD)

    pl.semaphore_wait(barrier, len(greeted))

    right_z, left_z = at(sx, sz + 1, sc, hy), at(sx, sz - 1, sc, hy)
    right_x, left_x = at(sx + 1, sz, sc, hy), at(sx - 1, sz, sc, hy)
    right_y, left_y = at(sx, sz, sc, hy + 1), at(sx, sz, sc, hy - 1)

    s_wz = Stream(wbuf.at[0, pl.ds(0, NZ - 1), 0])
    s_wx = Stream(wbuf.at[pl.ds(0, NX - 1), :, 0])
    s_wc = Stream(wbuf.at[:, :, 0])
    s_kz = Stream(kvb.at[pl.ds(0, NZ - 1), :, 0])
    s_kc = Stream(kvb.at[:, :, 0])
    wc_came, kc_came = new_sem(), new_sem()
    wx_came = {1: new_sem(), -1: new_sem()}

    def wz(step, way):
        origin = lax.rem(sz - way * (step - 1) + NZ, NZ)
        if step < NZ // 2:
            part = wbuf.at[sx, origin, sc]
        else:
            part = wbuf.at[sx, origin, sc, pl.ds(0 if way == 1 else 32, 32)]
        return s_wz.send(part, part, right_z if way == 1 else left_z, new_sem())

    def wx_first(origin):
        part = wbuf.at[sx, origin, sc]
        for way in (1, -1):
            s_wx.send(part, part, right_x if way == 1 else left_x, wx_came[way])

    def wx_second(way):
        part = wbuf.at[lax.rem(sx - way + NX, NX), pl.ds(0 if way == 1 else NZ // 2, NZ // 2), sc]
        return s_wx.send(part, part, right_x if way == 1 else left_x, new_sem())

    def kz(step, way, half):
        origin = lax.rem(sz - way * (step - 1) + NZ, NZ)
        part = kvb.at[kslot(origin), pl.ds(half * 2, 2), cc]
        return s_kz.send(part, part, right_z if way == 1 else left_z, new_sem())

    def w_sibling(part):
        s_wc.send(part, part, home, wc_came)

    def k_sibling(part):
        s_kc.send(part, part, home, kc_came)

    s_dec, dec_came = Stream(dec.at[pl.ds(0, GROUP - 1)]), new_sem()
    for i in farthest(GROUP):
        s_dec.send(dsr.at[group[i] // (GROUP // HEADS)], dec.at[p], group_dev[i], dec_came)
    dec[p] = dsr[p // (GROUP // HEADS)]
    s_st, st_came = Stream(rs.at[pl.ds(0, GROUP - 1)]), new_sem()
    for i in farthest(GROUP):
        s_st.send(st.at[group[i]], rs.at[p], group_dev[i], st_came)
    rs[p] = st[p]

    loads["w"].wait()
    c_wz = {(1, way): wz(1, way) for way in (1, -1)}

    def wz_step(step):
        for way in (1, -1):
            c_wz[step, way].wait_recv()
            if step < NZ // 2:
                c_wz[step + 1, way] = wz(step + 1, way)
    loads["q"].wait()
    for h in range(HEADS):
        lanes = slice(h * HD, (h + 1) * HD)
        spread = within[:, h:h + 1] - wrow[h:h + 1, :]
        factor = jnp.exp(jnp.where(lower, spread, -1e30))
        scores = dot(q[:, lanes], k[:, lanes], NT)
        intra[:, lanes] = dot((scores * factor).astype(BF16), v[:, lanes])

    loads["kw"].wait()
    c_swap = Stream(kin).send(kin, kvb.at[4 * (hy // 4) + lax.rem(sz, 4), swap_x, sc], swap_to, new_sem())
    loads["g"].wait()
    opened = g[...].astype(F32)
    acc[...] = opened / (1.0 + jnp.exp(-opened))

    arrived(dec.at[pl.ds(0, GROUP - 1)], dec_came)
    arrived(rs.at[pl.ds(0, GROUP - 1)], st_came)
    state = jnp.zeros((SLICE, HD), F32)
    passed = jnp.zeros((1, HD), F32)
    for i in range(GROUP):
        ex[i] = state
        step = dec[i]
        dec[i] = passed
        state = jnp.exp(step) * state + rs[i].astype(F32)
        passed = passed + step
    xs[sx, 0:SLICE, :] = state
    xs[sx, SLICE:SLICE + 8, :] = jnp.broadcast_to(passed, (8, HD))
    s_xs, xs_came = Stream(xs.at[pl.ds(0, NX - 1)]), new_sem()
    for i in farthest(NX):
        s_xs.send(xs.at[sx], xs.at[sx], cross_dev[i], xs_came)

    wz_step(1)

    arrived(xs.at[pl.ds(0, NX - 1)], xs_came)
    base = jnp.zeros((SLICE, HD), F32)
    for x in range(NX - 1):
        fresh = jnp.exp(xs[x, SLICE:SLICE + 1, :]) * base + xs[x, 0:SLICE, :]
        base = jnp.where(x < sx, fresh, base)
    s_inc, inc_came = Stream(ob.at[pl.ds(0, GROUP - 1)]), new_sem()
    for i in farthest(GROUP):
        there = group[i]
        ob[there] = (ex[there] + jnp.exp(dec[there]) * base).astype(BF16)
        s_inc.send(ob.at[there], inc.at[p], group_dev[i], inc_came)
    inc[p] = (ex[p] + jnp.exp(dec[p]) * base).astype(BF16)

    c_swap.wait_recv()
    own_kv = kvb.at[kslot(sz), sx, cc]
    s_kx, kx_came = Stream(kvb.at[0, pl.ds(0, NX - 1), 0]), new_sem()
    for i in farthest(NX):
        s_kx.send(own_kv, own_kv, cross_dev[i], kx_came)
    for step in (0, -1, 1):
        wx_first(lax.rem(sz + step + NZ, NZ))
    wz_step(2)
    for step in (-2, 2):
        wx_first(lax.rem(sz + step + NZ, NZ))
    wz_step(3)
    for step in (-3, 3):
        wx_first(lax.rem(sz + step + NZ, NZ))
    loads["r"].wait()
    arrived(kvb.at[0, pl.ds(0, NX - 1), 0], kx_came)
    arrived(inc.at[pl.ds(0, GROUP - 1)], inc_came)

    c_kz = {}
    c_wx = {}

    def kz_step(step, half):
        for way in (1, -1):
            if (step, way, half) not in c_kz:
                continue
            c_kz[step, way, half].wait_recv()
            if step + 1 < NZ // 2 or (step + 1 == NZ // 2 and half == (0 if way == 1 else 1)):
                c_kz[step + 1, way, half] = kz(step + 1, way, half)
            origin = lax.rem(sz - way * step + NZ, NZ)
            k_sibling(kvb.at[kslot(origin), pl.ds(half * 2, 2), cc])

    def wx_step(step):
        for way in (1, -1):
            origin = lax.rem(sx - way * step + NX, NX)
            if step == 1:
                arrived(wbuf.at[0, :, 0], wx_came[way])
                c_wx[way] = wx_second(way)
                w_sibling(wbuf.at[origin, :, sc])
            else:
                c_wx[way].wait_recv()
                half = pl.ds(0 if way == 1 else NZ // 2, NZ // 2)
                w_sibling(wbuf.at[origin, half, sc])

    s_mix, c_mix = Stream(abuf.at[pl.ds(0, NY - 1)]), {}

    def far(chunk):
        return 1 if chunk < CHUNKS // 2 else -1

    def mix_send(step, way, chunk):
        if step == NY // 2 and way != far(chunk):
            return
        origin = lax.rem(hy - way * (step - 1) + NY, NY)
        part = abuf.at[origin, pl.ds(chunk * ROWS, ROWS)]
        c_mix[step, way, chunk] = s_mix.send(part, part, right_y if way == 1 else left_y, new_sem())

    grown = jnp.exp(within)
    for chunk in ORDER:
        span = slice(chunk * ROWS, (chunk + 1) * ROWS)
        for h in range(HEADS):
            lanes = slice(h * HD, (h + 1) * HD)
            entering = inc[4 * h:4 * h + 4].reshape(HD, HD)
            kept = intra[span, lanes] + grown[span, h:h + 1] * dot(q[span, lanes], entering)
            scale = lax.rsqrt(jnp.mean(kept * kept, axis=1, keepdims=True) + 1e-6)
            abuf[hy, span, lanes] = (acc[span, lanes] * (kept * scale)).astype(BF16)
        for way in (1, -1):
            mix_send(1, way, chunk)
        if chunk < 2:
            for way in (1, -1):
                c_kz[1, way, chunk] = kz(1, way, chunk)

    wz_step(4)
    wx_first(lax.rem(sz + NZ // 2, NZ))
    w_sibling(wbuf.at[sx, :, sc])
    k_sibling(kvb.at[kslot(sz), :, cc])
    service = {
        0: (lambda: kz_step(1, 0),), 1: (lambda: kz_step(1, 1),),
        3: (lambda: kz_step(2, 0), lambda: wx_step(1)), 4: (lambda: kz_step(2, 1),),
        6: (lambda: kz_step(3, 0),), 7: (lambda: kz_step(3, 1),),
        9: (lambda: kz_step(4, 0), lambda: kz_step(4, 1), lambda: wx_step(2)),
    }
    for step in range(1, NY // 2):
        for n, chunk in enumerate(ORDER):
            for way in (1, -1):
                c_mix[step, way, chunk].wait_recv()
                mix_send(step + 1, way, chunk)
            for job in service.get((step - 1) * CHUNKS + n, ()):
                job()

    arrived(wbuf.at[:, :, 0], wc_came)

    def weight(origin):
        return wbuf[origin // 2, pl.ds(lax.rem(origin, 2) * 4, 4)].reshape(WID, WID)

    acc[...] = res[...].astype(F32)

    def projected(i, carry):
        origin = lax.rem(hy - (NY // 2 - 1) + i + NY, NY)
        acc[...] += dot(abuf[origin], weight(origin))
        return carry

    lax.fori_loop(0, NY - 1, projected, 0)
    arrived(kvb.at[:, :, 0], kc_came)

    last = lax.rem(hy + NY // 2, NY)
    s_red, c_red = Stream(red_out.at[pl.ds(0, NY - 1)]), {}

    def cache_weight(origin):
        return kvb[pl.ds(4 * (origin // 4), 4), lax.rem(origin, NX)].reshape(WID, 2 * HD)

    def toward(step, way):
        return lax.rem(hy + way * (NY // 2 - step) + NY, NY)

    def partial(origin, span):
        return dot(hg[span, :], cache_weight(origin))

    def side(way):
        return 0 if way == 1 else 1

    def rows_of(chunk):
        return slice(chunk * ROWS, (chunk + 1) * ROWS)

    def reduce_send(step, way, chunk, value):
        slot = step * 2 + side(way)
        if (step - 1, way, chunk) in c_red:
            c_red[step - 1, way, chunk].wait_recv()
            value = value + red_in[slot - 2, rows_of(chunk), :].astype(F32)
        red_out[slot, rows_of(chunk), :] = value.astype(BF16)
        c_red[step, way, chunk] = s_red.send(
            red_out.at[slot, pl.ds(chunk * ROWS, ROWS)], red_in.at[slot, pl.ds(chunk * ROWS, ROWS)],
            right_y if way == 1 else left_y, new_sem(),
        )

    gain = gain_ref[...].astype(F32).reshape(1, WID)
    for chunk in ORDER:
        span = rows_of(chunk)
        c_mix[NY // 2, far(chunk), chunk].wait_recv()
        hidden = (acc[span, :] + dot(abuf[last, span, :], weight(last))).astype(BF16).astype(F32)
        hg[span, :] = (hidden * gain).astype(BF16)
        scol[span, :] = jnp.broadcast_to(jnp.sum(hidden * hidden, axis=1, keepdims=True), (ROWS, HD))
        for step, way in ((0, far(chunk)), (1, -far(chunk))):
            reduce_send(step, way, chunk, partial(toward(step, way), span))
    for way in (1, -1):
        half = slice(0, TOK // 2) if way == 1 else slice(TOK // 2, TOK)
        part[side(way), half, :] = partial(toward(1, way), half)
    for chunk in ORDER:
        way = far(chunk)
        reduce_send(1, way, chunk, part[side(way), rows_of(chunk), :])
    sq[hy] = jnp.transpose(scol[...])[0:8, :]
    s_sq, sq_came = Stream(sq.at[pl.ds(0, NY - 1)]), new_sem()
    for i in farthest(NY):
        s_sq.send(sq.at[hy], sq.at[hy], head_dev[i], sq_came)
    for step in range(2, NY // 2):
        for way in (1, -1):
            part[side(way)] = partial(toward(step, way), slice(None))
        for late in (False, True):
            for chunk in ORDER:
                way = far(chunk) if late else -far(chunk)
                reduce_send(step, way, chunk, part[side(way), rows_of(chunk), :])
    part[0] = partial(hy, slice(None))
    arrived(sq.at[pl.ds(0, NY - 1)], sq_came)
    total = sq[0]
    for y in range(1, NY):
        total = total + sq[y]
    inverse = jnp.transpose(lax.rsqrt(total / (WID * NY) + 1e-6))
    for chunk in ORDER:
        span = rows_of(chunk)
        value = part[0, span, :]
        for way in (1, -1):
            c_red[NY // 2 - 1, way, chunk].wait_recv()
            value = value + red_in[NY - 2 + side(way), span, :].astype(F32)
        out_ref[span, :] = (value * inverse[span, 0:1]).astype(BF16)

    assert count[0] <= COPIES, count[0]
    for whole, sent in drains:
        pltpu.make_async_remote_copy(
            src_ref=whole, dst_ref=whole, send_sem=sent, recv_sem=sent,
            device_id=home, device_id_type=MESH,
        ).wait_send()


def on_device(queries, keys, values, gate, residual, log_decay, out_weight, norm_gain, kv_weight):
    hbm = pl.BlockSpec(memory_space=pltpu.HBM)
    vmem = pl.BlockSpec(memory_space=pltpu.VMEM)
    block = pltpu.VMEM((TOK, WID), BF16)
    reds = pltpu.VMEM((NY, TOK, 2 * HD), BF16)
    slices = pltpu.VMEM((GROUP, SLICE, HD), BF16)
    both = pl.pallas_call(
        layer_kernel,
        out_shape=jax.ShapeDtypeStruct((TOK, 2 * HD), BF16),
        in_specs=[hbm] * 5 + [vmem, hbm, vmem, hbm],
        out_specs=vmem,
        scratch_shapes=[
            block, block, block, block, block,
            pltpu.VMEM((NX, NZ, NC, 64, WID), BF16),
            pltpu.VMEM((NZ, NX, NC, 64, 2 * HD), BF16),
            pltpu.VMEM((64, 2 * HD), BF16),
            slices,
            slices,
            pltpu.VMEM((HEADS, 1, HD), F32),
            pltpu.VMEM((GROUP, 1, HD), F32),
            pltpu.VMEM((NX, SLICE + 8, HD), F32),
            pltpu.VMEM((GROUP, SLICE, HD), F32),
            slices,
            slices,
            pltpu.VMEM((TOK, WID), F32),
            pltpu.VMEM((NY, TOK, WID), BF16),
            pltpu.VMEM((TOK, WID), F32),
            block,
            reds, reds,
            pltpu.VMEM((2, TOK, 2 * HD), F32),
            pltpu.VMEM((TOK, HD), F32),
            pltpu.VMEM((NY, 8, TOK), F32),
            pltpu.SemaphoreType.DMA((7,)),
            pltpu.SemaphoreType.DMA((COPIES,)),
        ],
        compiler_params=pltpu.CompilerParams(
            collective_id=0, has_side_effects=True, vmem_limit_bytes=62 << 20
        ),
    )(
        queries, keys, values, gate, residual, log_decay.T, out_weight, norm_gain, kv_weight,
    )
    return both[:, :HD], both[:, HD:]


def solution(mesh):
    placed = (P("seq", "head"),) * 7 + (P("head"), P("seq", "head"))
    return jax.shard_map(
        on_device,
        mesh=mesh,
        in_specs=placed,
        out_specs=(P("seq", "head"), P("seq", "head")),
        check_vma=False,
    )
```
